256 devices in a mesh: row: 8 (over z_hi, core), col: 32 (over y, z_lo, x).
Axes of the slice: x: 4, y: 4, z: 8 (z_hi: 4, z_lo: 2; z = z_hi * 2 + z_lo), core: 2. Of those that a mesh axis runs over, the one named last changes fastest.
Arguments:
- features: bfloat16 [65536, 512], P('col'), may hold values from -6 to 6
- weight_raw: bfloat16 [512, 512], P('col'), may hold values from -0.0234375 to 0.0234375
- direction_raw: bfloat16 [512, 512], P('col'), may hold values from -0.0014648438 to 0.0014648438
- panel_index: int32 [4096], P('row'), may hold values from 0 to 65535, as said below
- labels: int32 [4096, 65536], P('row', 'col'), may hold values 0 or 1
Outputs:
- gradient: float32 [512, 512], P('col')
- hess_vec: float32 [512, 512], P('col')
The draws below stay inside these ranges and needn't reach their ends.
Inputs may be any that keep to these rules, and one draw needn't show every extreme that they name: `panel_index`: distinct compounds; the largest entry is 65535.
All inputs are finite; a program needn't handle non-finite values. No bound on the sum of `labels` on one device may be relied on, other than what follows from the above.
Results may differ from the reference program's by a relative error of at most 0.0033.
Values may be sent and summed in bfloat16 or wider, within the bound.
No kernel may reach another device: no remote copies, remote signals or barrier semaphores. Data moves between devices by JAX's collectives and lax.ppermute only.
A program may use at most 64 MiB of HBM per device.

```python
import math
import jax
import jax.numpy as jnp
from jax import lax

D = 512
COL_DEV = 2048
PANEL = 4096
COMPOUNDS = 65536
N_COL = 32


def draw_panel_index(key, part):
    order = jax.random.permutation(key, COMPOUNDS)
    chosen = order[:PANEL].astype(jnp.int32)
    return chosen + (COMPOUNDS - 1 - jnp.max(chosen))


def place_ends(array, stream_key, least, largest):
    longest = array.shape.index(max(array.shape))
    spots = []
    for shift in (0, 1):
        where = [jax.random.randint(jax.random.fold_in(stream_key, axis), (), 0, length) for axis, length in enumerate(array.shape)]
        where[longest] = (where[longest] + shift) % array.shape[longest]
        spots.append(tuple(where))
    return array.at[spots[0]].set(least).at[spots[1]].set(largest)


def with_spikes(values, own_key, source, target, parts, factor):
    owner, partner = [(jnp.arange(values.shape[dim]) // (values.shape[dim] // parts)).reshape([-1 if axis == dim else 1 for axis in range(values.ndim)]) for dim in (source, target)]
    chosen = jax.random.permutation(own_key, parts)[partner]
    strong = (owner == chosen) | (owner == (partner + parts // 2) % parts)
    return jnp.where(strong, factor * values, values)


def level_of(stream_key, shape, pieces, smallest, largest):
    def one(dim, parts):
        steps = jax.random.uniform(jax.random.fold_in(jax.random.fold_in(stream_key, 6), dim), (parts,), jnp.float32, smallest / len(pieces), largest / len(pieces))
        return jnp.repeat(jnp.exp(steps), shape[dim] // parts).reshape((-1,) + (1,) * (len(shape) - dim - 1))

    gain = one(*pieces[0])
    for cut in pieces[1:]:
        gain = gain * one(*cut)
    return gain


def centred(key, dims, width, reach, cuts=(), kind=jnp.bfloat16):
    gain = level_of(key, dims, cuts, -0.22, 0.18) if cuts else 1.0
    values = jax.random.normal(key, dims, jnp.float32) * width * gain
    return jnp.minimum(jnp.maximum(values, -reach), reach).astype(kind)


def gaussian_with(own_key, dims, width, reach, shards, heavy, kind=jnp.bfloat16):
    drawn = width * jax.random.normal(own_key, dims, jnp.float32)
    if shards:
        drawn = drawn * level_of(own_key, dims, shards, -0.22, 0.18)
    return jnp.clip(with_spikes(drawn, jax.random.fold_in(own_key, 3), *heavy), -reach, reach).astype(kind)


def setup_inputs(seed: int = 0) -> dict:
    arg_keys = jax.random.split(jax.random.key(seed), 6)
    return {
        "features": gaussian_with(arg_keys[0], (COMPOUNDS, D), 1.0, 6.0, ((0, 32),), (0, 1, 32, 2.75)),
        "weight_raw": centred(arg_keys[1], (D, D), (D * D // 4) ** -0.5, 0.0234375, ((0, 32),)),
        "direction_raw": centred(arg_keys[2], (D, D), (PANEL * COMPOUNDS // 16) ** -0.5, 0.0014648438, ((0, 32),)),
        "panel_index": draw_panel_index(jax.random.fold_in(arg_keys[5], 71), 0),
        "labels": place_ends((jax.random.randint(arg_keys[4], (PANEL, COMPOUNDS), 0, 4) < 1).astype(jnp.int32), jax.random.fold_in(arg_keys[4], 1), 0, 1),
    }


def symmetric(matrix):
    as_float = matrix.astype(jnp.float32)
    return ((as_float + as_float.T) * 0.5).astype(jnp.bfloat16)

def reference(features, weight_raw, direction_raw, panel_index, labels):
    weight_sym = symmetric(weight_raw)
    direction_sym = symmetric(direction_raw)
    panel_rows = jnp.take(features, panel_index, axis=0)
    proj_weight = jnp.dot(panel_rows, weight_sym, preferred_element_type=jnp.float32)
    proj_direction = jnp.dot(panel_rows, direction_sym, preferred_element_type=jnp.float32)
    projected = jnp.concatenate([proj_weight, proj_direction], axis=0).astype(jnp.bfloat16)

    def column_step(col_sums, block_index):
        begin = (block_index * COL_DEV).astype(jnp.int32)
        col_block = lax.dynamic_slice_in_dim(features, begin, COL_DEV, 0)
        label_block = lax.dynamic_slice_in_dim(labels, begin, COL_DEV, 1)
        pair_vals = lax.dot_general(projected, col_block, (((1,), (1,)), ((), ())), preferred_element_type=jnp.float32)
        margin = pair_vals[:PANEL]
        change = pair_vals[PANEL:]
        probability = jax.nn.sigmoid(margin)
        residual_weight = probability - label_block.astype(jnp.float32)
        curvature_weight = probability * (1.0 - probability) * change
        pair_weights = jnp.concatenate([residual_weight, curvature_weight], axis=0).astype(jnp.bfloat16)
        return (col_sums + jnp.dot(pair_weights, col_block, preferred_element_type=jnp.float32), None)
    zero_sums = jnp.zeros((2 * PANEL, D), jnp.float32)
    col_sums, _ = lax.scan(column_step, zero_sums, jnp.arange(N_COL, dtype=jnp.int32))
    panel_float = panel_rows.astype(jnp.float32)
    pair_scale = 1.0 / math.sqrt(PANEL * COMPOUNDS)
    grad_half = jnp.dot(panel_float.T, col_sums[:PANEL], preferred_element_type=jnp.float32, precision=lax.Precision.HIGHEST)
    curv_half = jnp.dot(panel_float.T, col_sums[PANEL:], preferred_element_type=jnp.float32, precision=lax.Precision.HIGHEST)
    gradient = (grad_half + grad_half.T) * (0.5 * pair_scale)
    hess_vec = (curv_half + curv_half.T) * (0.5 * pair_scale)
    return (gradient, hess_vec)
```

```python
import math

import jax
import jax.numpy as jnp
from jax import lax
from jax.sharding import PartitionSpec as P

ROUND_ROWS = 32


def symmetric(matrix):
    as_float = matrix.astype(jnp.float32)
    return ((as_float + as_float.T) * 0.5).astype(jnp.bfloat16)


def exchange_rows(value, mask, axis_size):
    return lax.ppermute(value, "row", [(i, i ^ mask) for i in range(axis_size)])


def gather_panel(features, panel_index, extra_rows):
    n_col = lax.axis_size("col")
    me = lax.axis_index("col")
    col_count = features.shape[0]
    count = panel_index.shape[0]
    owner = panel_index // col_count
    place = lax.iota(jnp.int32, count)
    earlier = (owner[:, None] == owner[None, :]) & (place[None, :] < place[:, None])
    rank = jnp.sum(earlier.astype(jnp.int32), axis=1)
    rounds = jnp.max(rank) // ROUND_ROWS + 1

    def own_rows(step):
        slot = rank - step * ROUND_ROWS
        chosen = (lax.iota(jnp.int32, ROUND_ROWS)[:, None] == slot[None, :]) & (owner == me)[None, :]
        local = jnp.sum(jnp.where(chosen, (panel_index - me * col_count)[None, :], 0), axis=1)
        return jnp.take(features, jnp.clip(local, 0, col_count - 1), axis=0)

    def spread(rows):
        sent = jnp.broadcast_to(rows[None], (n_col,) + rows.shape)
        return lax.all_to_all(sent, "col", 0, 0, tiled=True)

    def in_order(step, received):
        slot = rank - step * ROUND_ROWS
        wanted = jnp.where((slot >= 0) & (slot < ROUND_ROWS), owner * ROUND_ROWS + slot, -1)
        pick = (wanted[:, None] == lax.iota(jnp.int32, n_col * ROUND_ROWS)[None, :]).astype(jnp.bfloat16)
        flat = received.reshape(n_col * ROUND_ROWS, received.shape[-1])
        return jnp.dot(pick, flat, preferred_element_type=jnp.float32).astype(jnp.bfloat16)

    received = spread(jnp.concatenate([own_rows(0), extra_rows], axis=0))
    panel = in_order(0, received[:, :ROUND_ROWS])

    def another(state):
        step, rows = state
        return step + 1, rows + in_order(step, spread(own_rows(step)))

    _, panel = lax.while_loop(lambda state: state[0] < rounds, another, (jnp.int32(1), panel))
    return panel, received[:, ROUND_ROWS:]


def shards(features, weight_raw, direction_raw, panel_index, labels):
    n_row, n_col = lax.axis_size("row"), lax.axis_size("col")
    share = weight_raw.shape[0]
    dim = features.shape[1]
    col_count = features.shape[0]
    panel_count = panel_index.shape[0]
    panel_rows, matrices = gather_panel(
        features, panel_index, jnp.concatenate([weight_raw, direction_raw], axis=0)
    )
    weight_sym = symmetric(matrices[:, :share].reshape(dim, dim))
    direction_sym = symmetric(matrices[:, share:].reshape(dim, dim))
    proj_weight = jnp.dot(panel_rows, weight_sym, preferred_element_type=jnp.float32)
    proj_direction = jnp.dot(panel_rows, direction_sym, preferred_element_type=jnp.float32)
    projected = jnp.concatenate([proj_weight, proj_direction], axis=0).astype(jnp.bfloat16)
    pair_vals = lax.dot_general(
        projected, features, (((1,), (1,)), ((), ())), preferred_element_type=jnp.float32
    )
    margin = pair_vals[:panel_count]
    change = pair_vals[panel_count:]
    probability = jax.nn.sigmoid(margin)
    residual_weight = probability - labels.astype(jnp.float32)
    curvature_weight = probability * (1.0 - probability) * change
    pair_weights = jnp.concatenate([residual_weight, curvature_weight], axis=0).astype(jnp.bfloat16)
    col_sums = jnp.dot(pair_weights, features, preferred_element_type=jnp.float32)
    panel_float = panel_rows.astype(jnp.float32)
    pair_scale = 1.0 / math.sqrt(panel_count * n_row * col_count * n_col)
    highest = lax.Precision.HIGHEST
    grad_half = jnp.dot(
        panel_float.T, col_sums[:panel_count], preferred_element_type=jnp.float32, precision=highest
    )
    curv_half = jnp.dot(
        panel_float.T, col_sums[panel_count:], preferred_element_type=jnp.float32, precision=highest
    )
    grad_term = (grad_half + grad_half.T) * (0.5 * pair_scale)
    curv_term = (curv_half + curv_half.T) * (0.5 * pair_scale)
    first_core = lax.axis_index("row") % 2 == 0
    kept = jnp.where(first_core, grad_term, curv_term)
    given = jnp.where(first_core, curv_term, grad_term).astype(jnp.bfloat16)
    chip_sum = (kept + exchange_rows(given, 1, n_row).astype(jnp.float32)).astype(jnp.bfloat16)
    parts = lax.all_to_all(chip_sum.reshape(n_col, dim // n_col, dim), "col", 0, 0, tiled=True)
    mine = jnp.sum(parts.astype(jnp.float32), axis=0)
    near = mine + exchange_rows(mine, 2, n_row)
    far = exchange_rows(mine, 4, n_row) + exchange_rows(mine, 6, n_row)
    total = near + far
    other = exchange_rows(total, 1, n_row)
    gradient = jnp.where(first_core, total, other)
    hess_vec = jnp.where(first_core, other, total)
    return (gradient, hess_vec)


def solution(mesh):
    return jax.shard_map(
        shards,
        mesh=mesh,
        in_specs=(P("col", None), P("col", None), P("col", None), P("row"), P("row", "col")),
        out_specs=(P("col", None), P("col", None)),
        check_vma=False,
    )
```

```python
import functools
import math

import jax
import jax.numpy as jnp
from jax import lax
from jax.experimental import pallas as pl
from jax.experimental.pallas import tpu as pltpu
from jax.sharding import PartitionSpec as P

BF16, F32, I32 = jnp.bfloat16, jnp.float32, jnp.int32
ROUND_ROWS = 32
STEP_ROWS = 256

in_vmem = functools.partial(pl.BlockSpec, memory_space=pltpu.VMEM)
in_smem = functools.partial(pl.BlockSpec, memory_space=pltpu.SMEM)
in_place = functools.partial(pl.BlockSpec, memory_space=pl.ANY)
params = functools.partial(pltpu.CompilerParams, vmem_limit_bytes=48 << 20)


def rows_of(a, b):
    return jnp.dot(a, b, preferred_element_type=F32)


def exchange(value, mask):
    return lax.ppermute(value, "row", [(i, i ^ mask) for i in range(lax.axis_size("row"))])


def pack_rows(features, panel_row, extra_rows, step):
    n_col = lax.axis_size("col")
    col_count, dim = features.shape
    count = panel_row.shape[1]
    n_extra = 0 if extra_rows is None else extra_rows[0].shape[0]

    def body(step_ref, panel_ref, *refs):
        extra, (features_hbm, out, table, arrived) = refs[:-4], refs[-4:]
        load = pltpu.make_async_copy(features_hbm, table, arrived)
        load.start()
        place = jnp.broadcast_to(panel_ref[...], (8, count)) - lax.axis_index("col") * col_count
        owned = (place >= 0) & (place < col_count)
        lane = lax.broadcasted_iota(I32, (8, count), 1)
        running = owned.astype(I32)
        shift = 1
        while shift < count:
            running = running + jnp.where(lane >= shift, pltpu.roll(running, shift, axis=1), 0)
            shift *= 2
        slot = jnp.where(owned, running - 1 - step_ref[0] * ROUND_ROWS, -1)[:1]
        mine = slot == lax.broadcasted_iota(I32, (ROUND_ROWS, count), 0)
        wanted = jnp.sum(jnp.where(mine, place[:1] + 1, 0), axis=1, keepdims=True) - 1
        pick = (wanted == lax.broadcasted_iota(I32, (ROUND_ROWS, col_count), 1)).astype(F32).astype(BF16)
        load.wait()
        message = rows_of(pick, table[...]).astype(BF16)
        if extra:
            second = lax.axis_index("row") % 2 == 1
            mixed = jnp.where(second, extra[1][...].astype(F32), extra[0][...].astype(F32))
            message = jnp.concatenate([message, mixed.astype(BF16)], axis=0)
        for peer in range(n_col):
            out[peer] = message

    return pl.pallas_call(
        body,
        name="pack_rows",
        out_shape=jax.ShapeDtypeStruct((n_col, ROUND_ROWS + n_extra, dim), BF16),
        in_specs=[in_smem(), in_vmem()] + [in_vmem()] * (0 if extra_rows is None else 2) + [in_place()],
        out_specs=in_vmem(),
        scratch_shapes=[pltpu.VMEM((col_count, dim), BF16), pltpu.SemaphoreType.DMA(())],
        compiler_params=params(),
    )(step, panel_row, *(extra_rows or ()), features)


def rank_rows(panel_row, panel_column, col_count):
    count = panel_row.shape[1]
    bits = col_count.bit_length() - 1

    def body(row_ref, column_ref, where, rounds):
        owner_row = lax.shift_right_logical(row_ref[...], bits)
        owner = lax.shift_right_logical(column_ref[...], bits)
        before = lax.broadcasted_iota(I32, (count, count), 1) < lax.broadcasted_iota(I32, (count, count), 0)
        same = jnp.where(before & (owner == owner_row), 1, 0)
        rank = jnp.sum(same, axis=1, keepdims=True)
        lane = lax.broadcasted_iota(I32, (count, 128), 1)
        where[...] = jnp.where(lane == 0, owner, rank)
        rounds[0] = jnp.max(rank) // ROUND_ROWS + 1

    assert col_count == 1 << bits
    return pl.pallas_call(
        body,
        name="rank_rows",
        out_shape=(jax.ShapeDtypeStruct((count, 128), I32), jax.ShapeDtypeStruct((1,), I32)),
        in_specs=[in_vmem(), in_vmem()],
        out_specs=(in_vmem(), in_smem()),
        compiler_params=params(),
    )(panel_row, panel_column)


def ordered(where, received, step):
    n_col, _, dim = received.shape
    rank = where[:, 1:2] - step * ROUND_ROWS
    slot = jnp.where((rank >= 0) & (rank < ROUND_ROWS), where[:, :1] * ROUND_ROWS + rank, -1)
    pick = slot == lax.broadcasted_iota(I32, (where.shape[0], n_col * ROUND_ROWS), 1)
    return rows_of(pick.astype(F32).astype(BF16), received[:, :ROUND_ROWS, :].reshape(n_col * ROUND_ROWS, dim))


def add_round(where, received, panel, step):
    def body(step_ref, where_ref, received_ref, panel_ref, out):
        fresh = ordered(where_ref[...], received_ref[...], step_ref[0])
        out[...] = (panel_ref[...].astype(F32) + fresh).astype(BF16)

    return pl.pallas_call(
        body,
        name="add_round",
        out_shape=jax.ShapeDtypeStruct(panel.shape, BF16),
        in_specs=[in_smem(), in_vmem(), in_vmem(), in_vmem()],
        out_specs=in_vmem(),
        compiler_params=params(),
    )(step, where, received, panel)


def symmetric_matrix(received):
    dim = received.shape[2]

    def body(received_ref, out):
        raw = received_ref[:, ROUND_ROWS:, :].reshape(dim, dim).astype(F32)
        out[...] = ((raw + raw.T) * 0.5).astype(BF16)

    return pl.pallas_call(
        body,
        name="symmetric_matrix",
        out_shape=jax.ShapeDtypeStruct((dim, dim), BF16),
        in_specs=[in_vmem()],
        out_specs=in_vmem(),
        compiler_params=params(),
    )(received)


def pair_products(panel, kept_matrix, other_matrix, features, labels):
    count, dim = panel.shape
    col_count = features.shape[0]
    steps = count // STEP_ROWS

    def body(panel_ref, kept_ref, other_ref, features_ref, labels_hbm, kept, given, projected, sums, labels_ref, arrived):
        loads = []
        for i in range(steps):
            part = pl.ds(i * STEP_ROWS, STEP_ROWS)
            loads.append(pltpu.make_async_copy(labels_hbm.at[part], labels_ref.at[part], arrived.at[i]))
            loads[i].start()
        core = lax.axis_index("row") % 2
        rows = panel_ref[...]
        projected[core] = rows_of(rows, kept_ref[...]).astype(BF16)
        projected[1 - core] = rows_of(rows, other_ref[...]).astype(BF16)
        columns = features_ref[...]
        for i in range(steps):
            part = pl.ds(i * STEP_ROWS, STEP_ROWS)
            both = jnp.concatenate([projected[0, part], projected[1, part]], axis=0)
            pairs = lax.dot_general(both, columns, (((1,), (1,)), ((), ())), preferred_element_type=F32)
            loads[i].wait()
            probability = 1.0 / (1.0 + jnp.exp(-pairs[:STEP_ROWS]))
            residual = (probability - labels_ref[part].astype(F32)).astype(BF16)
            curvature = (probability * (1.0 - probability) * pairs[STEP_ROWS:]).astype(BF16)
            total = rows_of(jnp.concatenate([residual, curvature], axis=0), columns).astype(BF16)
            sums[0, part] = total[:STEP_ROWS]
            sums[1, part] = total[STEP_ROWS:]
        turned = rows.T
        for out, place in ((kept, core), (given, 1 - core)):
            half = rows_of(turned, sums[place])
            out[...] = (half + half.T).astype(out.dtype)

    return pl.pallas_call(
        body,
        name="pair_products",
        out_shape=(jax.ShapeDtypeStruct((dim, dim), F32), jax.ShapeDtypeStruct((dim, dim), BF16)),
        in_specs=[in_vmem()] * 4 + [in_place()],
        out_specs=(in_vmem(), in_vmem()),
        scratch_shapes=[
            pltpu.VMEM((2, count, dim), BF16),
            pltpu.VMEM((2, count, dim), BF16),
            pltpu.VMEM((count, col_count), I32),
            pltpu.SemaphoreType.DMA((steps,)),
        ],
        compiler_params=params(),
    )(panel, kept_matrix, other_matrix, features, labels)


def shards(features, weight_raw, direction_raw, panel_index, labels):
    n_row, n_col = lax.axis_size("row"), lax.axis_size("col")
    col_count, dim = features.shape
    count = panel_index.shape[0]
    panel_row = panel_index.reshape(1, count)
    first = jnp.zeros((1,), I32)
    sent = pack_rows(features, panel_row, (weight_raw, direction_raw), first)
    received = lax.all_to_all(sent, "col", 0, 0, tiled=True)
    where, rounds = rank_rows(panel_row, panel_index.reshape(count, 1), col_count)
    kept_matrix = symmetric_matrix(received)
    other_matrix = exchange(kept_matrix, 1)
    panel = add_round(where, received, jnp.zeros((count, dim), BF16), first)

    def another(state):
        step, rows = state
        fresh = lax.all_to_all(pack_rows(features, panel_row, None, step), "col", 0, 0, tiled=True)
        return step + 1, add_round(where, fresh, rows, step)

    _, panel = lax.while_loop(lambda state: state[0][0] < rounds[0], another, (first + 1, panel))
    kept, given = pair_products(panel, kept_matrix, other_matrix, features, labels)
    chip_sum = (kept + exchange(given, 1).astype(F32)).astype(BF16)
    parts = lax.all_to_all(chip_sum.reshape(n_col, dim // n_col, dim), "col", 0, 0, tiled=True)
    mine = jnp.sum(parts.astype(F32), axis=0)
    near = mine + exchange(mine, 2)
    scale = 0.5 / math.sqrt(count * n_row * col_count * n_col)
    total = (near + exchange(near, 6)) * scale
    other = exchange(total, 1)
    on_first = lax.axis_index("row") % 2 == 0
    return jnp.where(on_first, total, other), jnp.where(on_first, other, total)


def solution(mesh):
    return jax.shard_map(
        shards,
        mesh=mesh,
        in_specs=(P("col", None), P("col", None), P("col", None), P("row"), P("row", "col")),
        out_specs=(P("col", None), P("col", None)),
        check_vma=False,
    )
```

```python
import functools
import math

import jax
import jax.numpy as jnp
from jax import lax
from jax.experimental import pallas as pl
from jax.experimental.pallas import tpu as pltpu
from jax.sharding import PartitionSpec as P

BF16, F32, I32 = jnp.bfloat16, jnp.float32, jnp.int32
ROUND_ROWS = 32
STEP_ROWS = 256
LOADS = 4

in_vmem = functools.partial(pl.BlockSpec, memory_space=pltpu.VMEM)
in_smem = functools.partial(pl.BlockSpec, memory_space=pltpu.SMEM)
in_place = functools.partial(pl.BlockSpec, memory_space=pl.ANY)


def params(mebibytes=12):
    return pltpu.CompilerParams(vmem_limit_bytes=mebibytes << 20)


def rows_of(a, b):
    return jnp.dot(a, b, preferred_element_type=F32)


def exchange(value, mask):
    return lax.ppermute(value, "row", [(i, i ^ mask) for i in range(lax.axis_size("row"))])


def pack_rows(features, panel_row, extra_rows, step):
    n_col = lax.axis_size("col")
    col_count, dim = features.shape
    count = panel_row.shape[1]
    n_extra = extra_rows[0].shape[0] if extra_rows else 0
    chunk = col_count // LOADS
    bits = col_count.bit_length() - 1
    assert col_count == 1 << bits

    def body(step_ref, panel_ref, *refs):
        extra, (features_hbm, out, rounds, table, tail, arrived) = refs[:-6], refs[-6:]
        loads = []
        for i in range(LOADS):
            part = pl.ds(i * chunk, chunk)
            loads.append(pltpu.make_async_copy(features_hbm.at[part], table.at[part], arrived.at[i]))
            loads[i].start()
        for core, source in enumerate(extra):
            @pl.when(lax.axis_index("row") % 2 == core)
            def _():
                pltpu.make_async_copy(source, tail, arrived.at[LOADS]).start()
        owner = lax.shift_right_logical(jnp.broadcast_to(panel_ref[...], (n_col, count)), bits)
        held = (owner == lax.broadcasted_iota(I32, (n_col, count), 0)).astype(I32)
        rounds[0] = (jnp.max(jnp.sum(held, axis=1, keepdims=True)) - 1) // ROUND_ROWS + 1
        place = jnp.broadcast_to(panel_ref[...], (8, count)) - lax.axis_index("col") * col_count
        owned = (place >= 0) & (place < col_count)
        lane = lax.broadcasted_iota(I32, (8, count), 1)
        running = owned.astype(I32)
        shift = 1
        while shift < count:
            running = running + jnp.where(lane >= shift, pltpu.roll(running, shift, axis=1), 0)
            shift *= 2
        slot = jnp.where(owned, running - 1 - step_ref[0] * ROUND_ROWS, -1)[:1]
        mine = slot == lax.broadcasted_iota(I32, (ROUND_ROWS, count), 0)
        wanted = jnp.sum(jnp.where(mine, place[:1] + 1, 0), axis=1, keepdims=True) - 1
        lane = lax.broadcasted_iota(I32, (ROUND_ROWS, chunk), 1)
        rows = jnp.zeros((ROUND_ROWS, dim), F32)
        for i in range(LOADS):
            pick = (wanted - i * chunk == lane).astype(F32).astype(BF16)
            loads[i].wait()
            rows = rows + rows_of(pick, table[pl.ds(i * chunk, chunk)])
        message = rows.astype(BF16)
        if extra:
            pltpu.make_async_copy(extra[0], tail, arrived.at[LOADS]).wait()
            message = jnp.concatenate([message, tail[...]], axis=0)
        for peer in range(n_col):
            out[peer] = message

    return pl.pallas_call(
        body,
        name="pack_rows",
        out_shape=(
            jax.ShapeDtypeStruct((n_col, ROUND_ROWS + n_extra, dim), BF16),
            jax.ShapeDtypeStruct((1,), I32),
        ),
        in_specs=[in_smem(), in_vmem()] + [in_place()] * len(extra_rows) + [in_place()],
        out_specs=(in_vmem(), in_smem()),
        scratch_shapes=[
            pltpu.VMEM((col_count, dim), BF16),
            pltpu.VMEM((max(n_extra, 16), dim), BF16),
            pltpu.SemaphoreType.DMA((LOADS + 1,)),
        ],
        compiler_params=params(),
    )(step, panel_row, *extra_rows, features)


def picks(panel_row, panel_column, bits, step, n_slots):
    count = panel_column.shape[0]
    owner_row = lax.shift_right_logical(panel_row, bits)
    owner = lax.shift_right_logical(panel_column, bits)
    before = lax.broadcasted_iota(I32, (count, count), 1) < lax.broadcasted_iota(I32, (count, count), 0)
    rank = jnp.sum(jnp.where(before & (owner == owner_row), 1, 0), axis=1, keepdims=True) - step * ROUND_ROWS
    slot = jnp.where((rank >= 0) & (rank < ROUND_ROWS), owner * ROUND_ROWS + rank, -1)
    return (slot == lax.broadcasted_iota(I32, (count, n_slots), 1)).astype(F32).astype(BF16)


def first_picks(panel_row, panel_column, col_count):
    n_slots = lax.axis_size("col") * ROUND_ROWS

    def body(row_ref, column_ref, out):
        out[...] = picks(row_ref[...], column_ref[...], col_count.bit_length() - 1, 0, n_slots)

    return pl.pallas_call(
        body,
        name="first_picks",
        out_shape=jax.ShapeDtypeStruct((panel_row.shape[1], n_slots), BF16),
        in_specs=[in_vmem(), in_vmem()],
        out_specs=in_vmem(),
        compiler_params=params(),
        cost_estimate=pl.CostEstimate(flops=8_000_000_000, transcendentals=0, bytes_accessed=32_000_000),
    )(panel_row, panel_column)


def panel_part(received):
    n_col, _, dim = received.shape
    return received[:, :ROUND_ROWS, :].reshape(n_col * ROUND_ROWS, dim)


def first_rows(pick, received, later):
    def body(pick_ref, received_ref, later_ref, out):
        rows = rows_of(pick_ref[...], panel_part(received_ref[...]))
        out[...] = (rows + later_ref[...].astype(F32)).astype(BF16)

    return pl.pallas_call(
        body,
        name="first_rows",
        out_shape=jax.ShapeDtypeStruct((pick.shape[0], received.shape[2]), BF16),
        in_specs=[in_vmem(), in_vmem(), in_vmem()],
        out_specs=in_vmem(),
        compiler_params=params(),
    )(pick, received, later)


def add_round(panel_row, panel_column, bits, received, panel, step):
    n_slots = received.shape[0] * ROUND_ROWS

    def body(step_ref, row_ref, column_ref, received_ref, panel_ref, out):
        pick = picks(row_ref[...], column_ref[...], bits, step_ref[0], n_slots)
        out[...] = (panel_ref[...].astype(F32) + rows_of(pick, panel_part(received_ref[...]))).astype(BF16)

    return pl.pallas_call(
        body,
        name="add_round",
        out_shape=jax.ShapeDtypeStruct(panel.shape, BF16),
        in_specs=[in_smem(), in_vmem(), in_vmem(), in_vmem(), in_vmem()],
        out_specs=in_vmem(),
        compiler_params=params(),
    )(step, panel_row, panel_column, received, panel)


def symmetric_matrix(received):
    dim = received.shape[2]

    def body(received_ref, out):
        raw = received_ref[:, ROUND_ROWS:, :].reshape(dim, dim).astype(F32)
        out[...] = ((raw + raw.T) * 0.5).astype(BF16)

    return pl.pallas_call(
        body,
        name="symmetric_matrix",
        out_shape=jax.ShapeDtypeStruct((dim, dim), BF16),
        in_specs=[in_vmem()],
        out_specs=in_vmem(),
        compiler_params=params(),
    )(received)


def pair_products(panel, kept_matrix, other_matrix, features, labels):
    count, dim = panel.shape
    col_count = features.shape[0]
    steps = count // STEP_ROWS

    def body(panel_ref, kept_ref, other_ref, features_ref, labels_hbm, kept, given, projected, sums, labels_ref, arrived):
        loads = []
        for i in range(steps):
            part = pl.ds(i * STEP_ROWS, STEP_ROWS)
            loads.append(pltpu.make_async_copy(labels_hbm.at[part], labels_ref.at[part], arrived.at[i]))
            loads[i].start()
        core = lax.axis_index("row") % 2
        rows = panel_ref[...]
        projected[core] = rows_of(rows, kept_ref[...]).astype(BF16)
        projected[1 - core] = rows_of(rows, other_ref[...]).astype(BF16)
        columns = features_ref[...]
        for i in range(steps):
            part = pl.ds(i * STEP_ROWS, STEP_ROWS)
            both = jnp.concatenate([projected[0, part], projected[1, part]], axis=0)
            pairs = lax.dot_general(both, columns, (((1,), (1,)), ((), ())), preferred_element_type=F32)
            loads[i].wait()
            probability = 1.0 / (1.0 + jnp.exp(-pairs[:STEP_ROWS]))
            residual = (probability - labels_ref[part].astype(F32)).astype(BF16)
            curvature = (probability * (1.0 - probability) * pairs[STEP_ROWS:]).astype(BF16)
            total = rows_of(jnp.concatenate([residual, curvature], axis=0), columns).astype(BF16)
            sums[0, part] = total[:STEP_ROWS]
            sums[1, part] = total[STEP_ROWS:]
        turned = rows.T
        for out, place in ((kept, core), (given, 1 - core)):
            half = rows_of(turned, sums[place])
            out[...] = (half + half.T).astype(out.dtype)

    return pl.pallas_call(
        body,
        name="pair_products",
        out_shape=(jax.ShapeDtypeStruct((dim, dim), F32), jax.ShapeDtypeStruct((dim, dim), BF16)),
        in_specs=[in_vmem()] * 4 + [in_place()],
        out_specs=(in_vmem(), in_vmem()),
        scratch_shapes=[
            pltpu.VMEM((2, count, dim), BF16),
            pltpu.VMEM((2, count, dim), BF16),
            pltpu.VMEM((count, col_count), I32),
            pltpu.SemaphoreType.DMA((steps,)),
        ],
        compiler_params=params(28),
    )(panel, kept_matrix, other_matrix, features, labels)


def shards(features, weight_raw, direction_raw, panel_index, labels):
    n_row, n_col = lax.axis_size("row"), lax.axis_size("col")
    col_count, dim = features.shape
    count = panel_index.shape[0]
    columns = features
    features, weight_raw, direction_raw, labels = (
        pltpu.with_memory_space_constraint(x, pltpu.HBM) for x in (features, weight_raw, direction_raw, labels)
    )
    panel_row = panel_index.reshape(1, count)
    first = jnp.zeros((1,), I32)
    sent, rounds = pack_rows(features, panel_row, (weight_raw, direction_raw), first)

    def another(state):
        step, rows = state
        fresh = lax.all_to_all(pack_rows(features, panel_row, (), step)[0], "col", 0, 0, tiled=True)
        column = panel_index.reshape(count, 1)
        return step + 1, add_round(panel_row, column, col_count.bit_length() - 1, fresh, rows, step)

    _, later = lax.while_loop(
        lambda state: state[0][0] < rounds[0], another, (first + 1, jnp.zeros((count, dim), BF16))
    )
    sent, later = lax.optimization_barrier((sent, later))
    received = lax.all_to_all(sent, "col", 0, 0, tiled=True)
    pick = first_picks(panel_row, panel_index.reshape(count, 1), col_count)
    received, pick = lax.optimization_barrier((received, pick))
    kept_matrix = symmetric_matrix(received)
    other_matrix = exchange(kept_matrix, 1)
    panel = first_rows(pick, received, later)
    kept, given = pair_products(panel, kept_matrix, other_matrix, columns, labels)
    chip_sum = (kept + exchange(given, 1).astype(F32)).astype(BF16)
    parts = lax.all_to_all(chip_sum.reshape(n_col, dim // n_col, dim), "col", 0, 0, tiled=True)
    mine = jnp.sum(parts.astype(F32), axis=0)
    near = mine + exchange(mine, 2)
    scale = 0.5 / math.sqrt(count * n_row * col_count * n_col)
    total = (near + exchange(near, 6)) * scale
    other = exchange(total, 1)
    on_first = lax.axis_index("row") % 2 == 0
    return jnp.where(on_first, total, other), jnp.where(on_first, other, total)


def solution(mesh):
    return jax.shard_map(
        shards,
        mesh=mesh,
        in_specs=(P("col", None), P("col", None), P("col", None), P("row"), P("row", "col")),
        out_specs=(P("col", None), P("col", None)),
        check_vma=False,
    )
```

```python
import functools
import math

import jax
import jax.numpy as jnp
from jax import lax
from jax.experimental import pallas as pl
from jax.experimental.pallas import tpu as pltpu
from jax.sharding import PartitionSpec as P

BF16, F32, I32 = jnp.bfloat16, jnp.float32, jnp.int32
ROUND_ROWS = 32
STEP_COLUMNS = 512
LOADS = 4

in_vmem = functools.partial(pl.BlockSpec, memory_space=pltpu.VMEM)
in_smem = functools.partial(pl.BlockSpec, memory_space=pltpu.SMEM)
in_place = functools.partial(pl.BlockSpec, memory_space=pl.ANY)


def params(mebibytes=8):
    return pltpu.CompilerParams(vmem_limit_bytes=mebibytes << 20)


def rows_of(a, b):
    return jnp.dot(a, b, preferred_element_type=F32)


def exchange(value, mask):
    return lax.ppermute(value, "row", [(i, i ^ mask) for i in range(lax.axis_size("row"))])


def count_rounds(panel_row, col_count):
    n_col = lax.axis_size("col")
    count = panel_row.shape[1]
    bits = col_count.bit_length() - 1
    assert col_count == 1 << bits

    def body(row_ref, rounds):
        owner = lax.shift_right_logical(jnp.broadcast_to(row_ref[...], (n_col, count)), bits)
        held = (owner == lax.broadcasted_iota(I32, (n_col, count), 0)).astype(I32)
        rounds[0] = (jnp.max(jnp.sum(held, axis=1, keepdims=True)) - 1) // ROUND_ROWS + 1

    return pl.pallas_call(
        body,
        name="count_rounds",
        out_shape=jax.ShapeDtypeStruct((1,), I32),
        in_specs=[in_vmem()],
        out_specs=in_smem(),
        compiler_params=params(),
    )(panel_row)


def picks(panel_row, bits, step, n_slots):
    count = panel_row.shape[1]
    panel_column = jnp.broadcast_to(panel_row, (128, count)).T[:, :1]
    owner_row = lax.shift_right_logical(panel_row, bits)
    owner = lax.shift_right_logical(panel_column, bits)
    before = lax.broadcasted_iota(I32, (count, count), 1) < lax.broadcasted_iota(I32, (count, count), 0)
    rank = jnp.sum(jnp.where(before & (owner == owner_row), 1, 0), axis=1, keepdims=True) - step * ROUND_ROWS
    slot = jnp.where((rank >= 0) & (rank < ROUND_ROWS), owner * ROUND_ROWS + rank, -1)
    return (slot == lax.broadcasted_iota(I32, (count, n_slots), 1)).astype(F32).astype(BF16)


def pack_rows(features, panel_row, extra_rows, step):
    n_col = lax.axis_size("col")
    n_slots = n_col * ROUND_ROWS
    col_count, dim = features.shape
    count = panel_row.shape[1]
    n_extra = extra_rows[0].shape[0] if extra_rows else 0
    bits = col_count.bit_length() - 1
    assert col_count == 1 << bits
    chunk = col_count // LOADS

    def body(step_ref, row_ref, *refs):
        extra, (features_from, out, pick_out, table, tail, arrived) = refs[:-6], refs[-6:]
        loads = []
        for i in range(LOADS):
            part = pl.ds(i * chunk, chunk)
            loads.append(pltpu.make_async_copy(features_from.at[part], table.at[part], arrived.at[i]))
            loads[i].start()
        for core, source in enumerate(extra):
            @pl.when(lax.axis_index("row") % 2 == core)
            def _():
                pltpu.make_async_copy(source, tail, arrived.at[LOADS]).start()
        place = jnp.broadcast_to(row_ref[...], (8, count)) - lax.axis_index("col") * col_count
        owned = (place >= 0) & (place < col_count)
        lane = lax.broadcasted_iota(I32, (8, count), 1)
        running = owned.astype(I32)
        shift = 1
        while shift < count:
            running = running + jnp.where(lane >= shift, pltpu.roll(running, shift, axis=1), 0)
            shift *= 2
        slot = jnp.where(owned, running - 1 - step_ref[0] * ROUND_ROWS, -1)[:1]
        mine = slot == lax.broadcasted_iota(I32, (ROUND_ROWS, count), 0)
        wanted = jnp.sum(jnp.where(mine, place[:1] + 1, 0), axis=1, keepdims=True) - 1
        pick_out[...] = picks(row_ref[...], bits, step_ref[0], n_slots)
        lane = lax.broadcasted_iota(I32, (ROUND_ROWS, chunk), 1)
        rows = jnp.zeros((ROUND_ROWS, dim), F32)
        for i in range(LOADS):
            chosen = (wanted - i * chunk == lane).astype(F32).astype(BF16)
            loads[i].wait()
            rows = rows + rows_of(chosen, table[pl.ds(i * chunk, chunk)])
        message = rows.astype(BF16)
        if extra:
            pltpu.make_async_copy(extra[0], tail, arrived.at[LOADS]).wait()
            message = jnp.concatenate([message, tail[...]], axis=0)
        for peer in range(n_col):
            out[peer] = message

    return pl.pallas_call(
        body,
        name="pack_rows",
        out_shape=(
            jax.ShapeDtypeStruct((n_col, ROUND_ROWS + n_extra, dim), BF16),
            jax.ShapeDtypeStruct((count, n_slots), BF16),
            jax.ShapeDtypeStruct((col_count, dim), BF16),
        ),
        in_specs=[in_smem(), in_vmem()] + [in_place()] * len(extra_rows) + [in_place()],
        out_specs=(in_vmem(), in_vmem(), in_vmem()),
        scratch_shapes=[
            pltpu.VMEM((max(n_extra, 16), dim), BF16),
            pltpu.SemaphoreType.DMA((LOADS + 1,)),
        ],
        compiler_params=params(),
    )(step, panel_row, *extra_rows, features)


def panel_part(received):
    n_col, _, dim = received.shape
    return received[:, :ROUND_ROWS, :].reshape(n_col * ROUND_ROWS, dim)


def add_round(pick, received, panel):
    def body(pick_ref, received_ref, panel_ref, out):
        rows = rows_of(pick_ref[...], panel_part(received_ref[...]))
        out[...] = (panel_ref[...].astype(F32) + rows).astype(BF16)

    return pl.pallas_call(
        body,
        name="add_round",
        out_shape=jax.ShapeDtypeStruct(panel.shape, BF16),
        in_specs=[in_vmem(), in_vmem(), in_vmem()],
        out_specs=in_vmem(),
        compiler_params=params(),
    )(pick, received, panel)


def symmetric_matrix(received):
    dim = received.shape[2]

    def body(received_ref, out):
        raw = received_ref[:, ROUND_ROWS:, :].reshape(dim, dim).astype(F32)
        out[...] = ((raw + raw.T) * 0.5).astype(BF16)

    return pl.pallas_call(
        body,
        name="symmetric_matrix",
        out_shape=jax.ShapeDtypeStruct((dim, dim), BF16),
        in_specs=[in_vmem()],
        out_specs=in_vmem(),
        compiler_params=params(),
    )(received)


def pairs_of(rows, matrix, columns):
    projected = rows_of(rows, matrix).astype(BF16)
    return lax.dot_general(projected, columns, (((1,), (1,)), ((), ())), preferred_element_type=F32)


def panel_product(turned, weights, columns):
    half = rows_of(turned, rows_of(weights, columns).astype(BF16))
    return half + half.T


def own_pairs(pick, received, later, kept_matrix, columns, labels):
    count, dim = later.shape

    def body(pick_ref, received_ref, later_ref, matrix_ref, columns_ref, labels_hbm, panel, turned, pairs, labels_out, arrived):
        load = pltpu.make_async_copy(labels_hbm, labels_out, arrived)
        load.start()
        rows = rows_of(pick_ref[...], panel_part(received_ref[...]))
        panel[...] = (rows + later_ref[...].astype(F32)).astype(BF16)
        pairs[...] = pairs_of(panel[...], matrix_ref[...], columns_ref[...])
        turned[...] = panel[...].T
        load.wait()

    return pl.pallas_call(
        body,
        name="own_pairs",
        out_shape=(
            jax.ShapeDtypeStruct((count, dim), BF16),
            jax.ShapeDtypeStruct((dim, count), BF16),
            jax.ShapeDtypeStruct((count, columns.shape[0]), F32),
            jax.ShapeDtypeStruct(labels.shape, I32),
        ),
        in_specs=[in_vmem()] * 5 + [in_place()],
        out_specs=(in_vmem(),) * 4,
        scratch_shapes=[pltpu.SemaphoreType.DMA(())],
        compiler_params=params(),
    )(pick, received, later, kept_matrix, columns, labels)


def given_part(panel, turned, other_matrix, own, columns, labels):
    count, dim = panel.shape
    col_count = columns.shape[0]

    def body(panel_ref, turned_ref, matrix_ref, own_ref, columns_ref, labels_ref, given, kept_weights, weights):
        first = lax.axis_index("row") % 2 == 0
        projected = rows_of(panel_ref[...], matrix_ref[...]).astype(BF16)
        for start in range(0, col_count, STEP_COLUMNS):
            part = pl.ds(start, STEP_COLUMNS)
            other = lax.dot_general(
                projected, columns_ref[part], (((1,), (1,)), ((), ())), preferred_element_type=F32
            )
            mine = own_ref[:, part]
            margin = jnp.where(first, mine, other)
            change = jnp.where(first, other, mine)
            probability = 1.0 / (1.0 + jnp.exp(-margin))
            residual = probability - labels_ref[:, part].astype(F32)
            curvature = probability * (1.0 - probability) * change
            kept_weights[:, part] = jnp.where(first, residual, curvature).astype(BF16)
            weights[:, part] = jnp.where(first, curvature, residual).astype(BF16)
        given[...] = panel_product(turned_ref[...], weights[...], columns_ref[...]).astype(BF16)

    return pl.pallas_call(
        body,
        name="given_part",
        out_shape=(jax.ShapeDtypeStruct((dim, dim), BF16), jax.ShapeDtypeStruct((count, col_count), BF16)),
        in_specs=[in_vmem()] * 6,
        out_specs=(in_vmem(), in_vmem()),
        scratch_shapes=[pltpu.VMEM((count, col_count), BF16)],
        compiler_params=params(16),
    )(panel, turned, other_matrix, own, columns, labels)


def kept_part(turned, weights, columns):
    dim = columns.shape[1]

    def body(turned_ref, weights_ref, columns_ref, out):
        out[...] = panel_product(turned_ref[...], weights_ref[...], columns_ref[...])

    return pl.pallas_call(
        body,
        name="kept_part",
        out_shape=jax.ShapeDtypeStruct((dim, dim), F32),
        in_specs=[in_vmem()] * 3,
        out_specs=in_vmem(),
        compiler_params=params(),
    )(turned, weights, columns)


def shards(features, weight_raw, direction_raw, panel_index, labels):
    n_row, n_col = lax.axis_size("row"), lax.axis_size("col")
    col_count, dim = features.shape
    count = panel_index.shape[0]
    features, weight_raw, direction_raw, labels = (
        pltpu.with_memory_space_constraint(x, pltpu.HBM) for x in (features, weight_raw, direction_raw, labels)
    )
    panel_row = panel_index.reshape(1, count)
    first = jnp.zeros((1,), I32)
    rounds = count_rounds(panel_row, col_count)

    def another(state):
        step, rows = state
        message, pick, _ = pack_rows(features, panel_row, (), step)
        return step + 1, add_round(pick, lax.all_to_all(message, "col", 0, 0, tiled=True), rows)

    _, later = lax.while_loop(
        lambda state: state[0][0] < rounds[0], another, (first + 1, jnp.zeros((count, dim), BF16))
    )
    panel_row, later = lax.optimization_barrier((panel_row, later))
    sent, pick, columns = pack_rows(features, panel_row, (weight_raw, direction_raw), first)
    received = lax.all_to_all(sent, "col", 0, 0, tiled=True)
    kept_matrix = symmetric_matrix(received)
    other_matrix = exchange(kept_matrix, 1)
    panel, turned, own, labels = own_pairs(pick, received, later, kept_matrix, columns, labels)
    given, weights = given_part(panel, turned, other_matrix, own, columns, labels)
    swapped = exchange(given, 1)
    kept = kept_part(turned, weights, columns)
    chip_sum = (kept + swapped.astype(F32)).astype(BF16)
    parts = lax.all_to_all(chip_sum.reshape(n_col, dim // n_col, dim), "col", 0, 0, tiled=True)
    mine = jnp.sum(parts.astype(F32), axis=0)
    near = mine + exchange(mine, 2)
    scale = 0.5 / math.sqrt(count * n_row * col_count * n_col)
    total = (near + exchange(near, 6)) * scale
    other = exchange(total, 1)
    on_first = lax.axis_index("row") % 2 == 0
    return jnp.where(on_first, total, other), jnp.where(on_first, other, total)


def solution(mesh):
    return jax.shard_map(
        shards,
        mesh=mesh,
        in_specs=(P("col", None), P("col", None), P("col", None), P("row"), P("row", "col")),
        out_specs=(P("col", None), P("col", None)),
        check_vma=False,
    )
```

```python
import functools
import math

import jax
import jax.numpy as jnp
from jax import lax
from jax.experimental import pallas as pl
from jax.experimental.pallas import tpu as pltpu
from jax.sharding import PartitionSpec as P

BF16, F32, I32 = jnp.bfloat16, jnp.float32, jnp.int32
ROUND_ROWS = 32
STEP_COLUMNS = 512
LOADS = 4

in_vmem = functools.partial(pl.BlockSpec, memory_space=pltpu.VMEM)
in_smem = functools.partial(pl.BlockSpec, memory_space=pltpu.SMEM)
in_place = functools.partial(pl.BlockSpec, memory_space=pl.ANY)


def params(mebibytes=8):
    return pltpu.CompilerParams(vmem_limit_bytes=mebibytes << 20)


def rows_of(a, b):
    return jnp.dot(a, b, preferred_element_type=F32)


def exchange(value, mask):
    return lax.ppermute(value, "row", [(i, i ^ mask) for i in range(lax.axis_size("row"))])


def ranks(panel_row, bits):
    count = panel_row.shape[1]
    owner_row = lax.shift_right_logical(panel_row, bits)
    owner = jnp.broadcast_to(owner_row, (128, count)).T[:, :1]
    same = owner == owner_row
    down, along = (lax.broadcasted_iota(I32, (count, count), axis) for axis in (0, 1))
    rank_row = jnp.sum(jnp.where(same & (down < along), 1, 0), axis=0, keepdims=True)
    rank = jnp.sum(jnp.where(same & (along < down), 1, 0), axis=1, keepdims=True)
    return owner_row, rank_row, owner, rank


def own_places(panel_row, owner_row, rank_row, col_count, step):
    count = panel_row.shape[1]
    me = lax.axis_index("col")
    slot = jnp.where(owner_row == me, rank_row - step * ROUND_ROWS, -1)
    mine = slot == lax.broadcasted_iota(I32, (ROUND_ROWS, count), 0)
    return jnp.sum(jnp.where(mine, panel_row + (1 - me * col_count), 0), axis=1, keepdims=True) - 1


def load_columns(features, panel_row):
    col_count, dim = features.shape
    count = panel_row.shape[1]
    bits = col_count.bit_length() - 1
    chunk = col_count // LOADS
    assert col_count == 1 << bits

    def body(row_from, features_hbm, table, rounds, places, blank, row_ref, zeros, arrived):
        row_load = pltpu.make_async_copy(row_from, row_ref, arrived.at[LOADS + 1])
        row_load.start()
        loads = []
        for i in range(LOADS):
            part = pl.ds(i * chunk, chunk)
            loads.append(pltpu.make_async_copy(features_hbm.at[part], table.at[part], arrived.at[i]))
            loads[i].start()
        zeros[...] = jnp.zeros_like(zeros)
        loads.append(pltpu.make_async_copy(zeros, blank, arrived.at[LOADS]))
        loads[LOADS].start()
        row_load.wait()
        row = row_ref[...]
        owner_row, rank_row, _, _ = ranks(row, bits)
        rounds[0] = jnp.max(rank_row) // ROUND_ROWS + 1
        places[...] = jnp.broadcast_to(own_places(row, owner_row, rank_row, col_count, 0), (ROUND_ROWS, 128))
        for load in loads:
            load.wait()

    return pl.pallas_call(
        body,
        name="load_columns",
        out_shape=(
            jax.ShapeDtypeStruct(features.shape, BF16),
            jax.ShapeDtypeStruct((1,), I32),
            jax.ShapeDtypeStruct((ROUND_ROWS, 128), I32),
            jax.ShapeDtypeStruct((count, dim), BF16),
        ),
        in_specs=[in_place(), in_place()],
        out_specs=(in_vmem(), in_smem(), in_vmem(), in_place()),
        scratch_shapes=[
            pltpu.VMEM((1, count), I32),
            pltpu.VMEM((count, dim), BF16),
            pltpu.SemaphoreType.DMA((LOADS + 2,)),
        ],
        compiler_params=params(),
    )(panel_row, features)


def pack_rows(columns, panel_row, extra_rows, places, step):
    n_col = lax.axis_size("col")
    n_slots = n_col * ROUND_ROWS
    col_count, dim = columns.shape
    count = panel_row.shape[1]
    n_extra = extra_rows[0].shape[0] if extra_rows else 0
    bits = col_count.bit_length() - 1

    def body(step_ref, row_ref, columns_ref, places_ref, *refs):
        extra, (out, pick_out, tail, arrived) = refs[:-4], refs[-4:]
        for core, source in enumerate(extra):
            @pl.when(lax.axis_index("row") % 2 == core)
            def _():
                pltpu.make_async_copy(source, tail, arrived).start()
        row, step = row_ref[...], step_ref[0]
        owner_row, rank_row, owner, rank = ranks(row, bits)
        wanted = places_ref[:, :1] if extra else own_places(row, owner_row, rank_row, col_count, step)
        chosen = (wanted == lax.broadcasted_iota(I32, (ROUND_ROWS, col_count), 1)).astype(F32).astype(BF16)
        message = rows_of(chosen, columns_ref[...]).astype(BF16)
        rank = rank - step * ROUND_ROWS
        slot = jnp.where((rank >= 0) & (rank < ROUND_ROWS), owner * ROUND_ROWS + rank, -1)
        pick = slot == lax.broadcasted_iota(I32, (count, n_slots), 1)
        pick_out[...] = pick.astype(F32).astype(BF16)
        if extra:
            pltpu.make_async_copy(extra[0], tail, arrived).wait()
            message = jnp.concatenate([message, tail[...]], axis=0)
        for peer in range(n_col):
            out[peer] = message

    return pl.pallas_call(
        body,
        name="pack_rows",
        out_shape=(
            jax.ShapeDtypeStruct((n_col, ROUND_ROWS + n_extra, dim), BF16),
            jax.ShapeDtypeStruct((count, n_slots), BF16),
        ),
        in_specs=[in_smem(), in_vmem(), in_vmem(), in_vmem()] + [in_place()] * len(extra_rows),
        out_specs=(in_vmem(), in_vmem()),
        scratch_shapes=[pltpu.VMEM((max(n_extra, 16), dim), BF16), pltpu.SemaphoreType.DMA(())],
        compiler_params=params(),
    )(step, panel_row, columns, places, *extra_rows)


def panel_part(received):
    n_col, _, dim = received.shape
    return received[:, :ROUND_ROWS, :].reshape(n_col * ROUND_ROWS, dim)


def add_round(pick, received, panel):
    def body(pick_ref, received_ref, panel_ref, out):
        rows = rows_of(pick_ref[...], panel_part(received_ref[...]))
        out[...] = (panel_ref[...].astype(F32) + rows).astype(BF16)

    return pl.pallas_call(
        body,
        name="add_round",
        out_shape=jax.ShapeDtypeStruct(panel.shape, BF16),
        in_specs=[in_vmem(), in_vmem(), in_vmem()],
        out_specs=in_vmem(),
        compiler_params=params(),
    )(pick, received, panel)


def symmetric_matrix(received):
    dim = received.shape[2]

    def body(received_ref, out):
        raw = received_ref[:, ROUND_ROWS:, :].reshape(dim, dim).astype(F32)
        out[...] = ((raw + raw.T) * 0.5).astype(BF16)

    return pl.pallas_call(
        body,
        name="symmetric_matrix",
        out_shape=jax.ShapeDtypeStruct((dim, dim), BF16),
        in_specs=[in_vmem()],
        out_specs=in_vmem(),
        compiler_params=params(),
    )(received)


def pairs_of(rows, matrix, columns):
    projected = rows_of(rows, matrix).astype(BF16)
    return lax.dot_general(projected, columns, (((1,), (1,)), ((), ())), preferred_element_type=F32)


def panel_product(turned, weights, columns):
    half = rows_of(turned, rows_of(weights, columns).astype(BF16))
    return half + half.T


def own_pairs(pick, received, later, kept_matrix, columns, labels):
    count, dim = later.shape

    def body(pick_ref, received_ref, later_ref, matrix_ref, columns_ref, labels_hbm, panel, turned, pairs, labels_out, arrived):
        load = pltpu.make_async_copy(labels_hbm, labels_out, arrived)
        load.start()
        rows = rows_of(pick_ref[...], panel_part(received_ref[...]))
        panel[...] = (rows + later_ref[...].astype(F32)).astype(BF16)
        pairs[...] = pairs_of(panel[...], matrix_ref[...], columns_ref[...])
        turned[...] = panel[...].T
        load.wait()

    return pl.pallas_call(
        body,
        name="own_pairs",
        out_shape=(
            jax.ShapeDtypeStruct((count, dim), BF16),
            jax.ShapeDtypeStruct((dim, count), BF16),
            jax.ShapeDtypeStruct((count, columns.shape[0]), F32),
            jax.ShapeDtypeStruct(labels.shape, I32),
        ),
        in_specs=[in_vmem()] * 5 + [in_place()],
        out_specs=(in_vmem(),) * 4,
        scratch_shapes=[pltpu.SemaphoreType.DMA(())],
        compiler_params=params(),
    )(pick, received, later, kept_matrix, columns, labels)


def given_part(panel, turned, other_matrix, own, columns, labels):
    count, dim = panel.shape
    col_count = columns.shape[0]

    def body(panel_ref, turned_ref, matrix_ref, own_ref, columns_ref, labels_ref, given, kept_weights, weights):
        first = lax.axis_index("row") % 2 == 0
        projected = rows_of(panel_ref[...], matrix_ref[...]).astype(BF16)
        for start in range(0, col_count, STEP_COLUMNS):
            part = pl.ds(start, STEP_COLUMNS)
            other = lax.dot_general(
                projected, columns_ref[part], (((1,), (1,)), ((), ())), preferred_element_type=F32
            )
            mine = own_ref[:, part]
            margin = jnp.where(first, mine, other)
            change = jnp.where(first, other, mine)
            probability = 1.0 / (1.0 + jnp.exp(-margin))
            residual = probability - labels_ref[:, part].astype(F32)
            curvature = probability * (1.0 - probability) * change
            kept_weights[:, part] = jnp.where(first, residual, curvature).astype(BF16)
            weights[:, part] = jnp.where(first, curvature, residual).astype(BF16)
        given[...] = panel_product(turned_ref[...], weights[...], columns_ref[...]).astype(BF16)

    return pl.pallas_call(
        body,
        name="given_part",
        out_shape=(jax.ShapeDtypeStruct((dim, dim), BF16), jax.ShapeDtypeStruct((count, col_count), BF16)),
        in_specs=[in_vmem()] * 6,
        out_specs=(in_vmem(), in_vmem()),
        scratch_shapes=[pltpu.VMEM((count, col_count), BF16)],
        compiler_params=params(16),
    )(panel, turned, other_matrix, own, columns, labels)


def kept_part(turned, weights, columns):
    dim = columns.shape[1]

    def body(turned_ref, weights_ref, columns_ref, out):
        out[...] = panel_product(turned_ref[...], weights_ref[...], columns_ref[...])

    return pl.pallas_call(
        body,
        name="kept_part",
        out_shape=jax.ShapeDtypeStruct((dim, dim), F32),
        in_specs=[in_vmem()] * 3,
        out_specs=in_vmem(),
        compiler_params=params(),
    )(turned, weights, columns)


def shards(features, weight_raw, direction_raw, panel_index, labels):
    n_row, n_col = lax.axis_size("row"), lax.axis_size("col")
    col_count, dim = features.shape
    count = panel_index.shape[0]
    features, weight_raw, direction_raw, labels = (
        pltpu.with_memory_space_constraint(x, pltpu.HBM) for x in (features, weight_raw, direction_raw, labels)
    )
    panel_row = panel_index.reshape(1, count)
    first = jnp.zeros((1,), I32)
    columns, rounds, places, blank = load_columns(features, panel_row)

    def another(state):
        step, rows = state
        message, pick = pack_rows(columns, panel_row, (), places, step)
        return step + 1, add_round(pick, lax.all_to_all(message, "col", 0, 0, tiled=True), rows)

    _, later = lax.while_loop(lambda state: state[0][0] < rounds[0], another, (first + 1, blank))
    panel_row, later = lax.optimization_barrier((panel_row, later))
    columns = pltpu.with_memory_space_constraint(columns, pltpu.VMEM)
    sent, pick = pack_rows(columns, panel_row, (weight_raw, direction_raw), places, first)
    received = lax.all_to_all(sent, "col", 0, 0, tiled=True)
    kept_matrix = symmetric_matrix(received)
    other_matrix = exchange(kept_matrix, 1)
    panel, turned, own, labels = own_pairs(pick, received, later, kept_matrix, columns, labels)
    given, weights = given_part(panel, turned, other_matrix, own, columns, labels)
    swapped = exchange(given, 1)
    kept = kept_part(turned, weights, columns)
    chip_sum = (kept + swapped.astype(F32)).astype(BF16)
    parts = lax.all_to_all(chip_sum.reshape(n_col, dim // n_col, dim), "col", 0, 0, tiled=True)
    mine = jnp.sum(parts.astype(F32), axis=0)
    near = mine + exchange(mine, 2)
    scale = 0.5 / math.sqrt(count * n_row * col_count * n_col)
    total = (near + exchange(near, 6)) * scale
    other = exchange(total, 1)
    on_first = lax.axis_index("row") % 2 == 0
    return jnp.where(on_first, total, other), jnp.where(on_first, other, total)


def solution(mesh):
    return jax.shard_map(
        shards,
        mesh=mesh,
        in_specs=(P("col", None), P("col", None), P("col", None), P("row"), P("row", "col")),
        out_specs=(P("col", None), P("col", None)),
        check_vma=False,
    )
```

```python
import functools
import math

import jax
import jax.numpy as jnp
from jax import lax
from jax.experimental import pallas as pl
from jax.experimental.pallas import tpu as pltpu
from jax.sharding import PartitionSpec as P

BF16, F32, I32 = jnp.bfloat16, jnp.float32, jnp.int32
ROUND_ROWS = 32
STEP_COLUMNS = 256
LOADS = 4

in_vmem = functools.partial(pl.BlockSpec, memory_space=pltpu.VMEM)
in_smem = functools.partial(pl.BlockSpec, memory_space=pltpu.SMEM)
in_place = functools.partial(pl.BlockSpec, memory_space=pl.ANY)


def params(mebibytes=8):
    return pltpu.CompilerParams(vmem_limit_bytes=mebibytes << 20)


def rows_of(a, b):
    return jnp.dot(a, b, preferred_element_type=F32)


def exchange(value, mask):
    return lax.ppermute(value, "row", [(i, i ^ mask) for i in range(lax.axis_size("row"))])


def ranks(panel_row, bits):
    count = panel_row.shape[1]
    owner_row = lax.shift_right_logical(panel_row, bits)
    owner = jnp.broadcast_to(owner_row, (128, count)).T[:, :1]
    same = owner == owner_row
    down, along = (lax.broadcasted_iota(I32, (count, count), axis) for axis in (0, 1))
    rank_row = jnp.sum(jnp.where(same & (down < along), 1, 0), axis=0, keepdims=True)
    rank = jnp.sum(jnp.where(same & (along < down), 1, 0), axis=1, keepdims=True)
    return owner_row, rank_row, owner, rank


def own_places(panel_row, owner_row, rank_row, col_count, step):
    count = panel_row.shape[1]
    me = lax.axis_index("col")
    slot = jnp.where(owner_row == me, rank_row - step * ROUND_ROWS, -1)
    mine = slot == lax.broadcasted_iota(I32, (ROUND_ROWS, count), 0)
    return jnp.sum(jnp.where(mine, panel_row + (1 - me * col_count), 0), axis=1, keepdims=True) - 1


def load_columns(features, panel_row, matrices):
    col_count, dim = features.shape
    count = panel_row.shape[1]
    bits = col_count.bit_length() - 1
    chunk = col_count // LOADS
    assert col_count == 1 << bits

    def body(row_from, features_hbm, *refs):
        matrix_rows, (table, rounds, places, tail, blank, row_ref, zeros, arrived) = refs[:2], refs[2:]
        row_load = pltpu.make_async_copy(row_from, row_ref, arrived.at[LOADS + 1])
        row_load.start()
        loads = []
        for i in range(LOADS):
            part = pl.ds(i * chunk, chunk)
            loads.append(pltpu.make_async_copy(features_hbm.at[part], table.at[part], arrived.at[i]))
            loads[i].start()
        for core, source in enumerate(matrix_rows):
            @pl.when(lax.axis_index("row") % 2 == core)
            def _():
                pltpu.make_async_copy(source, tail, arrived.at[LOADS + 2]).start()
        zeros[...] = jnp.zeros_like(zeros)
        loads.append(pltpu.make_async_copy(zeros, blank, arrived.at[LOADS]))
        loads[LOADS].start()
        row_load.wait()
        row = row_ref[...]
        owner_row, rank_row, _, _ = ranks(row, bits)
        rounds[0] = jnp.max(rank_row) // ROUND_ROWS + 1
        places[...] = jnp.broadcast_to(own_places(row, owner_row, rank_row, col_count, 0), (ROUND_ROWS, 128))
        pltpu.make_async_copy(matrix_rows[0], tail, arrived.at[LOADS + 2]).wait()
        for load in loads:
            load.wait()

    return pl.pallas_call(
        body,
        name="load_columns",
        out_shape=(
            jax.ShapeDtypeStruct(features.shape, BF16),
            jax.ShapeDtypeStruct((1,), I32),
            jax.ShapeDtypeStruct((ROUND_ROWS, 128), I32),
            jax.ShapeDtypeStruct(matrices[0].shape, BF16),
            jax.ShapeDtypeStruct((count, dim), BF16),
        ),
        in_specs=[in_place()] * 4,
        out_specs=(in_vmem(), in_smem(), in_vmem(), in_vmem(), in_place()),
        scratch_shapes=[
            pltpu.VMEM((1, count), I32),
            pltpu.VMEM((count, dim), BF16),
            pltpu.SemaphoreType.DMA((LOADS + 3,)),
        ],
        compiler_params=params(),
    )(panel_row, features, *matrices)


def pack_rows(columns, panel_row, extra_rows, places, step):
    n_col = lax.axis_size("col")
    n_slots = n_col * ROUND_ROWS
    col_count, dim = columns.shape
    count = panel_row.shape[1]
    n_extra = extra_rows[0].shape[0] if extra_rows else 0
    bits = col_count.bit_length() - 1

    def body(step_ref, row_ref, columns_ref, places_ref, *refs):
        extra, (out, pick_out) = refs[:-2], refs[-2:]
        row, step = row_ref[...], step_ref[0]
        owner_row, rank_row, owner, rank = ranks(row, bits)
        wanted = places_ref[:, :1] if extra else own_places(row, owner_row, rank_row, col_count, step)
        chosen = (wanted == lax.broadcasted_iota(I32, (ROUND_ROWS, col_count), 1)).astype(F32).astype(BF16)
        message = rows_of(chosen, columns_ref[...]).astype(BF16)
        rank = rank - step * ROUND_ROWS
        slot = jnp.where((rank >= 0) & (rank < ROUND_ROWS), owner * ROUND_ROWS + rank, -1)
        pick = slot == lax.broadcasted_iota(I32, (count, n_slots), 1)
        pick_out[...] = pick.astype(F32).astype(BF16)
        if extra:
            message = jnp.concatenate([message, extra[0][...]], axis=0)
        for peer in range(n_col):
            out[peer] = message

    return pl.pallas_call(
        body,
        name="pack_rows",
        out_shape=(
            jax.ShapeDtypeStruct((n_col, ROUND_ROWS + n_extra, dim), BF16),
            jax.ShapeDtypeStruct((count, n_slots), BF16),
        ),
        in_specs=[in_smem()] + [in_vmem()] * (3 + len(extra_rows)),
        out_specs=(in_vmem(), in_vmem()),
        compiler_params=params(),
    )(step, panel_row, columns, places, *extra_rows)


def panel_part(received):
    n_col, _, dim = received.shape
    return received[:, :ROUND_ROWS, :].reshape(n_col * ROUND_ROWS, dim)


def add_round(pick, received, panel):
    def body(pick_ref, received_ref, panel_ref, out):
        rows = rows_of(pick_ref[...], panel_part(received_ref[...]))
        out[...] = (panel_ref[...].astype(F32) + rows).astype(BF16)

    return pl.pallas_call(
        body,
        name="add_round",
        out_shape=jax.ShapeDtypeStruct(panel.shape, BF16),
        in_specs=[in_vmem(), in_vmem(), in_vmem()],
        out_specs=in_vmem(),
        compiler_params=params(),
    )(pick, received, panel)


def symmetric_matrix(received):
    dim = received.shape[2]

    def body(received_ref, out):
        raw = received_ref[:, ROUND_ROWS:, :].reshape(dim, dim).astype(F32)
        out[...] = ((raw + raw.T) * 0.5).astype(BF16)

    return pl.pallas_call(
        body,
        name="symmetric_matrix",
        out_shape=jax.ShapeDtypeStruct((dim, dim), BF16),
        in_specs=[in_vmem()],
        out_specs=in_vmem(),
        compiler_params=params(),
    )(received)


def pairs_of(rows, matrix, columns):
    projected = rows_of(rows, matrix).astype(BF16)
    return lax.dot_general(projected, columns, (((1,), (1,)), ((), ())), preferred_element_type=F32)


def panel_product(turned, weights, columns):
    half = rows_of(turned, rows_of(weights, columns).astype(BF16))
    return half + half.T


def own_pairs(pick, received, later, kept_matrix, columns, labels):
    count, dim = later.shape

    def body(pick_ref, received_ref, later_ref, matrix_ref, columns_ref, labels_hbm, panel, turned, pairs, labels_out, arrived):
        load = pltpu.make_async_copy(labels_hbm, labels_out, arrived)
        load.start()
        rows = rows_of(pick_ref[...], panel_part(received_ref[...]))
        panel[...] = (rows + later_ref[...].astype(F32)).astype(BF16)
        pairs[...] = pairs_of(panel[...], matrix_ref[...], columns_ref[...])
        turned[...] = panel[...].T
        load.wait()

    return pl.pallas_call(
        body,
        name="own_pairs",
        out_shape=(
            jax.ShapeDtypeStruct((count, dim), BF16),
            jax.ShapeDtypeStruct((dim, count), BF16),
            jax.ShapeDtypeStruct((count, columns.shape[0]), F32),
            jax.ShapeDtypeStruct(labels.shape, I32),
        ),
        in_specs=[in_vmem()] * 5 + [in_place()],
        out_specs=(in_vmem(),) * 4,
        scratch_shapes=[pltpu.SemaphoreType.DMA(())],
        compiler_params=params(),
    )(pick, received, later, kept_matrix, columns, labels)


def given_part(panel, turned, other_matrix, own, columns, labels):
    count, dim = panel.shape
    col_count = columns.shape[0]

    def body(panel_ref, turned_ref, matrix_ref, own_ref, columns_ref, labels_ref, given, kept_weights, weights):
        first = lax.axis_index("row") % 2 == 0
        projected = rows_of(panel_ref[...], matrix_ref[...]).astype(BF16)
        for start in range(0, col_count, STEP_COLUMNS):
            part = pl.ds(start, STEP_COLUMNS)
            other = lax.dot_general(
                projected, columns_ref[part], (((1,), (1,)), ((), ())), preferred_element_type=F32
            )
            mine = own_ref[:, part]
            margin = jnp.where(first, mine, other)
            change = jnp.where(first, other, mine)
            probability = 1.0 / (1.0 + jnp.exp(-margin))
            residual = probability - labels_ref[:, part].astype(F32)
            curvature = probability * (1.0 - probability) * change
            kept_weights[:, part] = jnp.where(first, residual, curvature).astype(BF16)
            weights[:, part] = jnp.where(first, curvature, residual).astype(BF16)
        given[...] = panel_product(turned_ref[...], weights[...], columns_ref[...]).astype(BF16)

    return pl.pallas_call(
        body,
        name="given_part",
        out_shape=(jax.ShapeDtypeStruct((dim, dim), BF16), jax.ShapeDtypeStruct((count, col_count), BF16)),
        in_specs=[in_vmem()] * 6,
        out_specs=(in_vmem(), in_vmem()),
        scratch_shapes=[pltpu.VMEM((count, col_count), BF16)],
        compiler_params=params(16),
    )(panel, turned, other_matrix, own, columns, labels)


def kept_part(turned, weights, columns):
    dim = columns.shape[1]

    def body(turned_ref, weights_ref, columns_ref, out):
        out[...] = panel_product(turned_ref[...], weights_ref[...], columns_ref[...])

    return pl.pallas_call(
        body,
        name="kept_part",
        out_shape=jax.ShapeDtypeStruct((dim, dim), F32),
        in_specs=[in_vmem()] * 3,
        out_specs=in_vmem(),
        compiler_params=params(),
    )(turned, weights, columns)


def shards(features, weight_raw, direction_raw, panel_index, labels):
    n_row, n_col = lax.axis_size("row"), lax.axis_size("col")
    col_count, dim = features.shape
    count = panel_index.shape[0]
    features, weight_raw, direction_raw, labels = (
        pltpu.with_memory_space_constraint(x, pltpu.HBM) for x in (features, weight_raw, direction_raw, labels)
    )
    panel_row = panel_index.reshape(1, count)
    first = jnp.zeros((1,), I32)
    columns, rounds, places, matrix_rows, blank = load_columns(features, panel_row, (weight_raw, direction_raw))

    def another(state):
        step, rows = state
        message, pick = pack_rows(columns, panel_row, (), places, step)
        return step + 1, add_round(pick, lax.all_to_all(message, "col", 0, 0, tiled=True), rows)

    later = lax.cond(
        rounds[0] > 1,
        lambda rows: lax.while_loop(lambda state: state[0][0] < rounds[0], another, (first + 1, rows))[1],
        lambda rows: rows,
        blank,
    )
    panel_row, later = lax.optimization_barrier((panel_row, later))
    columns = pltpu.with_memory_space_constraint(columns, pltpu.VMEM)
    sent, pick = pack_rows(columns, panel_row, (matrix_rows,), places, first)
    received = lax.all_to_all(sent, "col", 0, 0, tiled=True)
    kept_matrix = symmetric_matrix(received)
    other_matrix = exchange(kept_matrix, 1)
    panel, turned, own, labels = own_pairs(pick, received, later, kept_matrix, columns, labels)
    given, weights = given_part(panel, turned, other_matrix, own, columns, labels)
    swapped = exchange(given, 1)
    kept = kept_part(turned, weights, columns)
    chip_sum = (kept + swapped.astype(F32)).astype(BF16)
    parts = lax.all_to_all(chip_sum.reshape(n_col, dim // n_col, dim), "col", 0, 0, tiled=True)
    mine = jnp.sum(parts.astype(F32), axis=0)
    near = mine + exchange(mine, 2)
    scale = 0.5 / math.sqrt(count * n_row * col_count * n_col)
    total = (near + exchange(near, 6)) * scale
    other = exchange(total, 1)
    on_first = lax.axis_index("row") % 2 == 0
    return jnp.where(on_first, total, other), jnp.where(on_first, other, total)


def solution(mesh):
    return jax.shard_map(
        shards,
        mesh=mesh,
        in_specs=(P("col", None), P("col", None), P("col", None), P("row"), P("row", "col")),
        out_specs=(P("col", None), P("col", None)),
        check_vma=False,
    )
```

```python
import functools
import math

import jax
import jax.numpy as jnp
from jax import lax
from jax.experimental import pallas as pl
from jax.experimental.pallas import tpu as pltpu
from jax.sharding import PartitionSpec as P

BF16, F32, I32 = jnp.bfloat16, jnp.float32, jnp.int32
ROUND_ROWS = 32
STEP_COLUMNS = 256
LOADS = 4

in_vmem = functools.partial(pl.BlockSpec, memory_space=pltpu.VMEM)
in_smem = functools.partial(pl.BlockSpec, memory_space=pltpu.SMEM)
in_place = functools.partial(pl.BlockSpec, memory_space=pl.ANY)


def params(mebibytes=8):
    return pltpu.CompilerParams(vmem_limit_bytes=mebibytes << 20)


def rows_of(a, b):
    return jnp.dot(a, b, preferred_element_type=F32)


def exchange(value, mask):
    return lax.ppermute(value, "row", [(i, i ^ mask) for i in range(lax.axis_size("row"))])


def ranks(panel_row, bits):
    count = panel_row.shape[1]
    owner_row = lax.shift_right_logical(panel_row, bits)
    owner = jnp.broadcast_to(owner_row, (128, count)).T[:, :1]
    same = owner == owner_row
    down, along = (lax.broadcasted_iota(I32, (count, count), axis) for axis in (0, 1))
    rank_row = jnp.sum(jnp.where(same & (down < along), 1, 0), axis=0, keepdims=True)
    rank = jnp.sum(jnp.where(same & (along < down), 1, 0), axis=1, keepdims=True)
    return owner_row, rank_row, owner, rank


def own_places(panel_row, owner_row, rank_row, col_count, step):
    count = panel_row.shape[1]
    me = lax.axis_index("col")
    slot = jnp.where(owner_row == me, rank_row - step * ROUND_ROWS, -1)
    mine = slot == lax.broadcasted_iota(I32, (ROUND_ROWS, count), 0)
    return jnp.sum(jnp.where(mine, panel_row + (1 - me * col_count), 0), axis=1, keepdims=True) - 1


def load_columns(features, panel_row, matrices):
    col_count, dim = features.shape
    count = panel_row.shape[1]
    bits = col_count.bit_length() - 1
    chunk = col_count // LOADS
    assert col_count == 1 << bits

    def body(row_from, features_hbm, *refs):
        matrix_rows, (table, rounds, places, where, tail, blank, row_ref, zeros, arrived) = refs[:2], refs[2:]
        row_load = pltpu.make_async_copy(row_from, row_ref, arrived.at[LOADS + 1])
        row_load.start()
        loads = []
        for i in range(LOADS):
            part = pl.ds(i * chunk, chunk)
            loads.append(pltpu.make_async_copy(features_hbm.at[part], table.at[part], arrived.at[i]))
            loads[i].start()
        for core, source in enumerate(matrix_rows):
            @pl.when(lax.axis_index("row") % 2 == core)
            def _():
                pltpu.make_async_copy(source, tail, arrived.at[LOADS + 2]).start()
        zeros[...] = jnp.zeros_like(zeros)
        loads.append(pltpu.make_async_copy(zeros, blank, arrived.at[LOADS]))
        loads[LOADS].start()
        row_load.wait()
        row = row_ref[...]
        owner_row, rank_row, owner, rank = ranks(row, bits)
        where[...] = jnp.where(lax.broadcasted_iota(I32, (count, 128), 1) == 0, owner, rank)
        rounds[0] = jnp.max(rank_row) // ROUND_ROWS + 1
        places[...] = jnp.broadcast_to(own_places(row, owner_row, rank_row, col_count, 0), (ROUND_ROWS, 128))
        pltpu.make_async_copy(matrix_rows[0], tail, arrived.at[LOADS + 2]).wait()
        for load in loads:
            load.wait()

    return pl.pallas_call(
        body,
        name="load_columns",
        out_shape=(
            jax.ShapeDtypeStruct(features.shape, BF16),
            jax.ShapeDtypeStruct((1,), I32),
            jax.ShapeDtypeStruct((ROUND_ROWS, 128), I32),
            jax.ShapeDtypeStruct((count, 128), I32),
            jax.ShapeDtypeStruct(matrices[0].shape, BF16),
            jax.ShapeDtypeStruct((count, dim), BF16),
        ),
        in_specs=[in_place()] * 4,
        out_specs=(in_vmem(), in_smem(), in_vmem(), in_vmem(), in_vmem(), in_place()),
        scratch_shapes=[
            pltpu.VMEM((1, count), I32),
            pltpu.VMEM((count, dim), BF16),
            pltpu.SemaphoreType.DMA((LOADS + 3,)),
        ],
        compiler_params=params(),
    )(panel_row, features, *matrices)


def pack_rows(columns, panel_row, extra_rows, places, where, step):
    n_col = lax.axis_size("col")
    n_slots = n_col * ROUND_ROWS
    col_count, dim = columns.shape
    count = panel_row.shape[1]
    n_extra = extra_rows[0].shape[0] if extra_rows else 0
    bits = col_count.bit_length() - 1

    def body(step_ref, row_ref, columns_ref, places_ref, where_ref, *refs):
        extra, (out, pick_out) = refs[:-2], refs[-2:]
        step = step_ref[0]
        if extra:
            wanted = places_ref[:, :1]
        else:
            owner_row, rank_row, _, _ = ranks(row_ref[...], bits)
            wanted = own_places(row_ref[...], owner_row, rank_row, col_count, step)
        chosen = (wanted == lax.broadcasted_iota(I32, (ROUND_ROWS, col_count), 1)).astype(F32).astype(BF16)
        message = rows_of(chosen, columns_ref[...]).astype(BF16)
        owner, rank = where_ref[:, :1], where_ref[:, 1:2] - step * ROUND_ROWS
        slot = jnp.where((rank >= 0) & (rank < ROUND_ROWS), owner * ROUND_ROWS + rank, -1)
        pick = slot == lax.broadcasted_iota(I32, (count, n_slots), 1)
        pick_out[...] = pick.astype(F32).astype(BF16)
        if extra:
            message = jnp.concatenate([message, extra[0][...]], axis=0)
        for peer in range(n_col):
            out[peer] = message

    return pl.pallas_call(
        body,
        name="pack_rows",
        out_shape=(
            jax.ShapeDtypeStruct((n_col, ROUND_ROWS + n_extra, dim), BF16),
            jax.ShapeDtypeStruct((count, n_slots), BF16),
        ),
        in_specs=[in_smem()] + [in_vmem()] * (4 + len(extra_rows)),
        out_specs=(in_vmem(), in_vmem()),
        compiler_params=params(),
    )(step, panel_row, columns, places, where, *extra_rows)


def panel_part(received):
    n_col, _, dim = received.shape
    return received[:, :ROUND_ROWS, :].reshape(n_col * ROUND_ROWS, dim)


def add_round(pick, received, panel):
    def body(pick_ref, received_ref, panel_ref, out):
        rows = rows_of(pick_ref[...], panel_part(received_ref[...]))
        out[...] = (panel_ref[...].astype(F32) + rows).astype(BF16)

    return pl.pallas_call(
        body,
        name="add_round",
        out_shape=jax.ShapeDtypeStruct(panel.shape, BF16),
        in_specs=[in_vmem(), in_vmem(), in_vmem()],
        out_specs=in_vmem(),
        compiler_params=params(),
    )(pick, received, panel)


def symmetric_matrix(received):
    dim = received.shape[2]

    def body(received_ref, out):
        raw = received_ref[:, ROUND_ROWS:, :].reshape(dim, dim).astype(F32)
        out[...] = ((raw + raw.T) * 0.5).astype(BF16)

    return pl.pallas_call(
        body,
        name="symmetric_matrix",
        out_shape=jax.ShapeDtypeStruct((dim, dim), BF16),
        in_specs=[in_vmem()],
        out_specs=in_vmem(),
        compiler_params=params(),
    )(received)


def pairs_of(rows, matrix, columns):
    projected = rows_of(rows, matrix).astype(BF16)
    return lax.dot_general(projected, columns, (((1,), (1,)), ((), ())), preferred_element_type=F32)


def panel_product(turned, weights, columns):
    half = rows_of(turned, rows_of(weights, columns).astype(BF16))
    return half + half.T


def own_pairs(pick, received, later, kept_matrix, columns, labels):
    count, dim = later.shape

    def body(pick_ref, received_ref, later_ref, matrix_ref, columns_ref, labels_hbm, panel, turned, pairs, labels_out, arrived):
        load = pltpu.make_async_copy(labels_hbm, labels_out, arrived)
        load.start()
        rows = rows_of(pick_ref[...], panel_part(received_ref[...]))
        panel[...] = (rows + later_ref[...].astype(F32)).astype(BF16)
        pairs[...] = pairs_of(panel[...], matrix_ref[...], columns_ref[...])
        turned[...] = panel[...].T
        load.wait()

    return pl.pallas_call(
        body,
        name="own_pairs",
        out_shape=(
            jax.ShapeDtypeStruct((count, dim), BF16),
            jax.ShapeDtypeStruct((dim, count), BF16),
            jax.ShapeDtypeStruct((count, columns.shape[0]), F32),
            jax.ShapeDtypeStruct(labels.shape, I32),
        ),
        in_specs=[in_vmem()] * 5 + [in_place()],
        out_specs=(in_vmem(),) * 4,
        scratch_shapes=[pltpu.SemaphoreType.DMA(())],
        compiler_params=params(),
    )(pick, received, later, kept_matrix, columns, labels)


def given_part(panel, turned, other_matrix, own, columns, labels):
    count, dim = panel.shape
    col_count = columns.shape[0]

    def body(panel_ref, turned_ref, matrix_ref, own_ref, columns_ref, labels_ref, given, kept_weights, weights):
        first = lax.axis_index("row") % 2 == 0
        projected = rows_of(panel_ref[...], matrix_ref[...]).astype(BF16)
        for start in range(0, col_count, STEP_COLUMNS):
            part = pl.ds(start, STEP_COLUMNS)
            other = lax.dot_general(
                projected, columns_ref[part], (((1,), (1,)), ((), ())), preferred_element_type=F32
            )
            mine = own_ref[:, part]
            margin = jnp.where(first, mine, other)
            change = jnp.where(first, other, mine)
            probability = 1.0 / (1.0 + jnp.exp(-margin))
            residual = probability - labels_ref[:, part].astype(F32)
            curvature = probability * (1.0 - probability) * change
            kept_weights[:, part] = jnp.where(first, residual, curvature).astype(BF16)
            weights[:, part] = jnp.where(first, curvature, residual).astype(BF16)
        given[...] = panel_product(turned_ref[...], weights[...], columns_ref[...]).astype(BF16)

    return pl.pallas_call(
        body,
        name="given_part",
        out_shape=(jax.ShapeDtypeStruct((dim, dim), BF16), jax.ShapeDtypeStruct((count, col_count), BF16)),
        in_specs=[in_vmem()] * 6,
        out_specs=(in_vmem(), in_vmem()),
        scratch_shapes=[pltpu.VMEM((count, col_count), BF16)],
        compiler_params=params(16),
    )(panel, turned, other_matrix, own, columns, labels)


def kept_part(turned, weights, columns):
    dim = columns.shape[1]

    def body(turned_ref, weights_ref, columns_ref, out):
        out[...] = panel_product(turned_ref[...], weights_ref[...], columns_ref[...])

    return pl.pallas_call(
        body,
        name="kept_part",
        out_shape=jax.ShapeDtypeStruct((dim, dim), F32),
        in_specs=[in_vmem()] * 3,
        out_specs=in_vmem(),
        compiler_params=params(),
    )(turned, weights, columns)


def shards(features, weight_raw, direction_raw, panel_index, labels):
    n_row, n_col = lax.axis_size("row"), lax.axis_size("col")
    col_count, dim = features.shape
    count = panel_index.shape[0]
    features, weight_raw, direction_raw, labels = (
        pltpu.with_memory_space_constraint(x, pltpu.HBM) for x in (features, weight_raw, direction_raw, labels)
    )
    panel_row = panel_index.reshape(1, count)
    first = jnp.zeros((1,), I32)
    columns, rounds, places, where, matrix_rows, blank = load_columns(features, panel_row, (weight_raw, direction_raw))

    def another(state):
        step, rows = state
        message, pick = pack_rows(columns, panel_row, (), places, where, step)
        return step + 1, add_round(pick, lax.all_to_all(message, "col", 0, 0, tiled=True), rows)

    later = lax.cond(
        rounds[0] > 1,
        lambda rows: lax.while_loop(lambda state: state[0][0] < rounds[0], another, (first + 1, rows))[1],
        lambda rows: rows,
        blank,
    )
    panel_row, later = lax.optimization_barrier((panel_row, later))
    columns = pltpu.with_memory_space_constraint(columns, pltpu.VMEM)
    sent, pick = pack_rows(columns, panel_row, (matrix_rows,), places, where, first)
    received = lax.all_to_all(sent, "col", 0, 0, tiled=True)
    kept_matrix = symmetric_matrix(received)
    other_matrix = exchange(kept_matrix, 1)
    panel, turned, own, labels = own_pairs(pick, received, later, kept_matrix, columns, labels)
    given, weights = given_part(panel, turned, other_matrix, own, columns, labels)
    swapped = exchange(given, 1)
    kept = kept_part(turned, weights, columns)
    chip_sum = (kept + swapped.astype(F32)).astype(BF16)
    parts = lax.all_to_all(chip_sum.reshape(n_col, dim // n_col, dim), "col", 0, 0, tiled=True)
    mine = jnp.sum(parts.astype(F32), axis=0)
    near = mine + exchange(mine, 2)
    scale = 0.5 / math.sqrt(count * n_row * col_count * n_col)
    total = (near + exchange(near, 6)) * scale
    other = exchange(total, 1)
    on_first = lax.axis_index("row") % 2 == 0
    return jnp.where(on_first, total, other), jnp.where(on_first, other, total)


def solution(mesh):
    return jax.shard_map(
        shards,
        mesh=mesh,
        in_specs=(P("col", None), P("col", None), P("col", None), P("row"), P("row", "col")),
        out_specs=(P("col", None), P("col", None)),
        check_vma=False,
    )
```

```python
import functools
import math

import jax
import jax.numpy as jnp
from jax import lax
from jax.experimental import pallas as pl
from jax.experimental.pallas import tpu as pltpu
from jax.sharding import PartitionSpec as P

BF16, F32, I32 = jnp.bfloat16, jnp.float32, jnp.int32
ROUND_ROWS = 32
STEP_ROWS = 256
LOADS = 4

in_vmem = functools.partial(pl.BlockSpec, memory_space=pltpu.VMEM)
in_smem = functools.partial(pl.BlockSpec, memory_space=pltpu.SMEM)
in_place = functools.partial(pl.BlockSpec, memory_space=pl.ANY)


def params(mebibytes=8):
    return pltpu.CompilerParams(vmem_limit_bytes=mebibytes << 20)


def rows_of(a, b):
    return jnp.dot(a, b, preferred_element_type=F32)


def exchange(value, mask):
    return lax.ppermute(value, "row", [(i, i ^ mask) for i in range(lax.axis_size("row"))])


def ranks(panel_row, bits):
    count = panel_row.shape[1]
    owner_row = lax.shift_right_logical(panel_row, bits)
    owner = jnp.broadcast_to(owner_row, (128, count)).T[:, :1]
    same = owner == owner_row
    down, along = (lax.broadcasted_iota(I32, (count, count), axis) for axis in (0, 1))
    rank_row = jnp.sum(jnp.where(same & (down < along), 1, 0), axis=0, keepdims=True)
    rank = jnp.sum(jnp.where(same & (along < down), 1, 0), axis=1, keepdims=True)
    return owner_row, rank_row, owner, rank


def own_places(panel_row, owner_row, rank_row, col_count, step):
    count = panel_row.shape[1]
    me = lax.axis_index("col")
    slot = jnp.where(owner_row == me, rank_row - step * ROUND_ROWS, -1)
    mine = slot == lax.broadcasted_iota(I32, (ROUND_ROWS, count), 0)
    return jnp.sum(jnp.where(mine, panel_row + (1 - me * col_count), 0), axis=1, keepdims=True) - 1


def load_columns(features, panel_row, matrices):
    col_count, dim = features.shape
    count = panel_row.shape[1]
    bits = col_count.bit_length() - 1
    chunk = col_count // LOADS
    assert col_count == 1 << bits

    def body(row_from, features_hbm, *refs):
        matrix_rows, (table, rounds, places, where, tail, blank, row_ref, zeros, arrived) = refs[:2], refs[2:]
        row_load = pltpu.make_async_copy(row_from, row_ref, arrived.at[LOADS + 1])
        row_load.start()
        loads = []
        for i in range(LOADS):
            part = pl.ds(i * chunk, chunk)
            loads.append(pltpu.make_async_copy(features_hbm.at[part], table.at[part], arrived.at[i]))
            loads[i].start()
        for core, source in enumerate(matrix_rows):
            @pl.when(lax.axis_index("row") % 2 == core)
            def _():
                pltpu.make_async_copy(source, tail, arrived.at[LOADS + 2]).start()
        zeros[...] = jnp.zeros_like(zeros)
        loads.append(pltpu.make_async_copy(zeros, blank, arrived.at[LOADS]))
        loads[LOADS].start()
        row_load.wait()
        row = row_ref[...]
        owner_row, rank_row, owner, rank = ranks(row, bits)
        where[...] = jnp.where(lax.broadcasted_iota(I32, (count, 128), 1) == 0, owner, rank)
        rounds[0] = jnp.max(rank_row) // ROUND_ROWS + 1
        places[...] = jnp.broadcast_to(own_places(row, owner_row, rank_row, col_count, 0), (ROUND_ROWS, 128))
        pltpu.make_async_copy(matrix_rows[0], tail, arrived.at[LOADS + 2]).wait()
        for load in loads:
            load.wait()

    return pl.pallas_call(
        body,
        name="load_columns",
        out_shape=(
            jax.ShapeDtypeStruct(features.shape, BF16),
            jax.ShapeDtypeStruct((1,), I32),
            jax.ShapeDtypeStruct((ROUND_ROWS, 128), I32),
            jax.ShapeDtypeStruct((count, 128), I32),
            jax.ShapeDtypeStruct(matrices[0].shape, BF16),
            jax.ShapeDtypeStruct((count, dim), BF16),
        ),
        in_specs=[in_place()] * 4,
        out_specs=(in_vmem(), in_smem(), in_vmem(), in_vmem(), in_vmem(), in_place()),
        scratch_shapes=[
            pltpu.VMEM((1, count), I32),
            pltpu.VMEM((count, dim), BF16),
            pltpu.SemaphoreType.DMA((LOADS + 3,)),
        ],
        compiler_params=params(),
    )(panel_row, features, *matrices)


def pack_rows(columns, panel_row, extra_rows, places, where, step):
    n_col = lax.axis_size("col")
    n_slots = n_col * ROUND_ROWS
    col_count, dim = columns.shape
    count = panel_row.shape[1]
    n_extra = extra_rows[0].shape[0] if extra_rows else 0
    bits = col_count.bit_length() - 1

    def body(step_ref, row_ref, columns_ref, places_ref, where_ref, *refs):
        extra, (out, pick_out) = refs[:-2], refs[-2:]
        step = step_ref[0]
        if extra:
            wanted = places_ref[:, :1]
        else:
            owner_row, rank_row, _, _ = ranks(row_ref[...], bits)
            wanted = own_places(row_ref[...], owner_row, rank_row, col_count, step)
        chosen = (wanted == lax.broadcasted_iota(I32, (ROUND_ROWS, col_count), 1)).astype(F32).astype(BF16)
        message = rows_of(chosen, columns_ref[...]).astype(BF16)
        owner, rank = where_ref[:, :1], where_ref[:, 1:2] - step * ROUND_ROWS
        slot = jnp.where((rank >= 0) & (rank < ROUND_ROWS), owner * ROUND_ROWS + rank, -1)
        pick = slot == lax.broadcasted_iota(I32, (count, n_slots), 1)
        pick_out[...] = pick.astype(F32).astype(BF16)
        if extra:
            message = jnp.concatenate([message, extra[0][...]], axis=0)
        for peer in range(n_col):
            out[peer] = message

    return pl.pallas_call(
        body,
        name="pack_rows",
        out_shape=(
            jax.ShapeDtypeStruct((n_col, ROUND_ROWS + n_extra, dim), BF16),
            jax.ShapeDtypeStruct((count, n_slots), BF16),
        ),
        in_specs=[in_smem()] + [in_vmem()] * (4 + len(extra_rows)),
        out_specs=(in_vmem(), in_vmem()),
        compiler_params=params(),
    )(step, panel_row, columns, places, where, *extra_rows)


def panel_part(received):
    n_col, _, dim = received.shape
    return received[:, :ROUND_ROWS, :].reshape(n_col * ROUND_ROWS, dim)


def add_round(pick, received, panel):
    def body(pick_ref, received_ref, panel_ref, out):
        rows = rows_of(pick_ref[...], panel_part(received_ref[...]))
        out[...] = (panel_ref[...].astype(F32) + rows).astype(BF16)

    return pl.pallas_call(
        body,
        name="add_round",
        out_shape=jax.ShapeDtypeStruct(panel.shape, BF16),
        in_specs=[in_vmem(), in_vmem(), in_vmem()],
        out_specs=in_vmem(),
        compiler_params=params(),
    )(pick, received, panel)


def symmetric_matrix(received):
    dim = received.shape[2]

    def body(received_ref, out):
        raw = received_ref[:, ROUND_ROWS:, :].reshape(dim, dim).astype(F32)
        out[...] = ((raw + raw.T) * 0.5).astype(BF16)

    return pl.pallas_call(
        body,
        name="symmetric_matrix",
        out_shape=jax.ShapeDtypeStruct((dim, dim), BF16),
        in_specs=[in_vmem()],
        out_specs=in_vmem(),
        compiler_params=params(),
    )(received)


def pairs_of(rows, matrix, columns):
    projected = rows_of(rows, matrix).astype(BF16)
    return lax.dot_general(projected, columns, (((1,), (1,)), ((), ())), preferred_element_type=F32)


def panel_product(turned, weights, columns):
    half = rows_of(turned, rows_of(weights, columns).astype(BF16))
    return half + half.T


def own_pairs(pick, received, later, kept_matrix, columns, labels):
    count, dim = later.shape

    def body(pick_ref, received_ref, later_ref, matrix_ref, columns_ref, labels_hbm, panel, turned, pairs, labels_out, arrived):
        load = pltpu.make_async_copy(labels_hbm, labels_out, arrived)
        load.start()
        rows = rows_of(pick_ref[...], panel_part(received_ref[...]))
        panel[...] = (rows + later_ref[...].astype(F32)).astype(BF16)
        pairs[...] = pairs_of(panel[...], matrix_ref[...], columns_ref[...])
        turned[...] = panel[...].T
        load.wait()

    return pl.pallas_call(
        body,
        name="own_pairs",
        out_shape=(
            jax.ShapeDtypeStruct((count, dim), BF16),
            jax.ShapeDtypeStruct((dim, count), BF16),
            jax.ShapeDtypeStruct((count, columns.shape[0]), F32),
            jax.ShapeDtypeStruct(labels.shape, I32),
        ),
        in_specs=[in_vmem()] * 5 + [in_place()],
        out_specs=(in_vmem(),) * 4,
        scratch_shapes=[pltpu.SemaphoreType.DMA(())],
        compiler_params=params(),
    )(pick, received, later, kept_matrix, columns, labels)


def given_part(panel, turned, other_matrix, own, columns, labels):
    count, dim = panel.shape
    col_count = columns.shape[0]

    def body(panel_ref, turned_ref, matrix_ref, own_ref, columns_ref, labels_ref, given, kept_weights, sums):
        first = lax.axis_index("row") % 2 == 0
        projected = rows_of(panel_ref[...], matrix_ref[...]).astype(BF16)
        columns = columns_ref[...]
        for start in range(0, count, STEP_ROWS):
            part = pl.ds(start, STEP_ROWS)
            other = lax.dot_general(
                projected[start : start + STEP_ROWS], columns, (((1,), (1,)), ((), ())), preferred_element_type=F32
            )
            mine = own_ref[part]
            margin = jnp.where(first, mine, other)
            change = jnp.where(first, other, mine)
            probability = 1.0 / (1.0 + jnp.exp(-margin))
            residual = probability - labels_ref[part].astype(F32)
            curvature = probability * (1.0 - probability) * change
            kept_weights[part] = jnp.where(first, residual, curvature).astype(BF16)
            sums[part] = rows_of(jnp.where(first, curvature, residual).astype(BF16), columns).astype(BF16)
        half = rows_of(turned_ref[...], sums[...])
        given[...] = (half + half.T).astype(BF16)

    return pl.pallas_call(
        body,
        name="given_part",
        out_shape=(jax.ShapeDtypeStruct((dim, dim), BF16), jax.ShapeDtypeStruct((count, col_count), BF16)),
        in_specs=[in_vmem()] * 6,
        out_specs=(in_vmem(), in_vmem()),
        scratch_shapes=[pltpu.VMEM((count, dim), BF16)],
        compiler_params=params(16),
    )(panel, turned, other_matrix, own, columns, labels)


def kept_part(turned, weights, columns):
    dim = columns.shape[1]

    def body(turned_ref, weights_ref, columns_ref, out):
        out[...] = panel_product(turned_ref[...], weights_ref[...], columns_ref[...])

    return pl.pallas_call(
        body,
        name="kept_part",
        out_shape=jax.ShapeDtypeStruct((dim, dim), F32),
        in_specs=[in_vmem()] * 3,
        out_specs=in_vmem(),
        compiler_params=params(),
    )(turned, weights, columns)


def shards(features, weight_raw, direction_raw, panel_index, labels):
    n_row, n_col = lax.axis_size("row"), lax.axis_size("col")
    col_count, dim = features.shape
    count = panel_index.shape[0]
    features, weight_raw, direction_raw, labels = (
        pltpu.with_memory_space_constraint(x, pltpu.HBM) for x in (features, weight_raw, direction_raw, labels)
    )
    panel_row = panel_index.reshape(1, count)
    first = jnp.zeros((1,), I32)
    columns, rounds, places, where, matrix_rows, blank = load_columns(features, panel_row, (weight_raw, direction_raw))

    def another(state):
        step, rows = state
        message, pick = pack_rows(columns, panel_row, (), places, where, step)
        return step + 1, add_round(pick, lax.all_to_all(message, "col", 0, 0, tiled=True), rows)

    later = lax.cond(
        rounds[0] > 1,
        lambda rows: lax.while_loop(lambda state: state[0][0] < rounds[0], another, (first + 1, rows))[1],
        lambda rows: rows,
        blank,
    )
    panel_row, later = lax.optimization_barrier((panel_row, later))
    columns = pltpu.with_memory_space_constraint(columns, pltpu.VMEM)
    sent, pick = pack_rows(columns, panel_row, (matrix_rows,), places, where, first)
    received = lax.all_to_all(sent, "col", 0, 0, tiled=True)
    kept_matrix = symmetric_matrix(received)
    other_matrix = exchange(kept_matrix, 1)
    panel, turned, own, labels = own_pairs(pick, received, later, kept_matrix, columns, labels)
    given, weights = given_part(panel, turned, other_matrix, own, columns, labels)
    swapped = exchange(given, 1)
    kept = kept_part(turned, weights, columns)
    chip_sum = (kept + swapped.astype(F32)).astype(BF16)
    parts = lax.all_to_all(chip_sum.reshape(n_col, dim // n_col, dim), "col", 0, 0, tiled=True)
    mine = jnp.sum(parts.astype(F32), axis=0)
    near = mine + exchange(mine, 2)
    scale = 0.5 / math.sqrt(count * n_row * col_count * n_col)
    total = (near + exchange(near, 6)) * scale
    other = exchange(total, 1)
    on_first = lax.axis_index("row") % 2 == 0
    return jnp.where(on_first, total, other), jnp.where(on_first, other, total)


def solution(mesh):
    return jax.shard_map(
        shards,
        mesh=mesh,
        in_specs=(P("col", None), P("col", None), P("col", None), P("row"), P("row", "col")),
        out_specs=(P("col", None), P("col", None)),
        check_vma=False,
    )
```
